512 devices in a mesh: rows: 8 (over x_lo, y), cols: 64 (over z, x_hi, core).
Axes of the slice: x: 4 (x_hi: 2, x_lo: 2; x = x_hi * 2 + x_lo), y: 4, z: 16, core: 2. Of those that a mesh axis runs over, the one named last changes fastest.
Arguments:
- points: bfloat16 [32, 16384], P(None, ('rows', 'cols')), may hold values from 0 to 1
- samples: bfloat16 [32, 32768], P(None, 'cols'), may hold values from -0.5 to 1.5
- potential: float32 [32768], P('cols'), may hold values from -6 to 60
Outputs:
- point_potential: float32 [16384], P(('rows', 'cols'))
- sample_potential: float32 [32768], P('cols')
- barycenter: float32 [32, 16384], P(None, ('rows', 'cols'))
The draws below stay inside these ranges and needn't reach their ends.
All inputs are finite; a program needn't handle non-finite values.
Results may differ from the reference program's by a relative error of at most 0.00055.
Values may be sent and summed in bfloat16 or wider, within the bound.
No kernel may reach another device: no remote copies, remote signals or barrier semaphores. Data moves between devices by JAX's collectives and lax.ppermute only.
A program may use at most 64 MiB of HBM per device.

```python
import math
import jax
import jax.numpy as jnp
from jax import lax

DIM = 32
SM_DEV = 512
NPTS = 16384
NSAMP = 32768
N_ROWS = 8
N_COLS = 64


def draw_potential(key, part):
    level_key, order_key, jitter_key = jax.random.split(key, 3)
    block_count = NSAMP // SM_DEV
    order = jax.random.permutation(order_key, block_count).astype(jnp.float32)
    offset = jax.random.uniform(level_key, (block_count,), jnp.float32)
    levels = -1.0 + 56.0 * (order + offset) / block_count
    jitter = 3.0 * jnp.clip(jax.random.normal(jitter_key, (block_count, SM_DEV), jnp.float32), -2.0, 2.0)
    values = jnp.clip(levels[:, None] + jitter, -6.0, 60.0)
    return values.reshape(NSAMP)


def block_levels(key, extent, pieces, smallest, high):
    level, own = 1.0, jax.random.fold_in(key, 6)
    for position, parts in pieces:
        heights = jnp.exp(jax.random.uniform(jax.random.fold_in(own, position), (parts,), jnp.float32, smallest / len(pieces), high / len(pieces)))
        level = level * jnp.repeat(heights, extent[position] // parts).reshape([-1 if axis == position else 1 for axis in range(len(extent))])
    return level


def setup_inputs(seed: int = 0) -> dict:
    key_of = jax.random.split(jax.random.key(seed), 4)
    return {
        "points": jnp.clip(1.0 * jax.random.uniform(key_of[0], (DIM, NPTS), jnp.float32) ** block_levels(key_of[0], (DIM, NPTS), ((1, 512),), -0.2, 0.2), 0.0, 1.0).astype(jnp.bfloat16),
        "samples": jnp.clip(-0.5 + 2.0 * jax.random.uniform(key_of[1], (DIM, NSAMP), jnp.float32) ** block_levels(key_of[1], (DIM, NSAMP), ((1, 64),), -0.2, 0.2), -0.5, 1.5).astype(jnp.bfloat16),
        "potential": draw_potential(jax.random.fold_in(key_of[3], 71), 0),
    }


EPS = 0.25


def cost_block(block, samples, sample_sq):
    xf = block.astype(jnp.float32)
    point_sq = jnp.sum(xf * xf, axis=0)
    cross = lax.dot_general(block, samples, (((0,), (0,)), ((), ())), preferred_element_type=jnp.float32)
    return 0.5 * point_sq[:, None] + 0.5 * sample_sq[None, :] - cross


def reference(points, samples, potential):
    yf = samples.astype(jnp.float32)
    sample_sq = jnp.sum(yf * yf, axis=0)
    blocks = points.reshape(DIM, N_ROWS, NPTS // N_ROWS).transpose(1, 0, 2)

    def row_pass(block):
        cost = cost_block(block, samples, sample_sq)
        score = (potential[None, :] - cost) / EPS
        top = jnp.max(score, axis=1)
        total = jnp.sum(jnp.exp(score - top[:, None]), axis=1)
        return -EPS * (top + jnp.log(total) - math.log(NSAMP))

    point_potential = lax.map(row_pass, blocks)

    def col_pass(pair):
        block, fpart = pair
        cost = cost_block(block, samples, sample_sq)
        score = (fpart[:, None] - cost) / EPS
        top = jnp.max(score, axis=0)
        total = jnp.sum(jnp.exp(score - top[None, :]), axis=0)
        return top, total

    tops, totals = lax.map(col_pass, (blocks, point_potential))
    best = jnp.max(tops, axis=0)
    whole = jnp.sum(totals * jnp.exp(tops - best[None, :]), axis=0)
    sample_potential = -EPS * (best + jnp.log(whole) - math.log(NPTS))

    sample_blocks = samples.reshape(DIM, N_COLS, SM_DEV).transpose(1, 0, 2)
    sq_blocks = sample_sq.reshape(N_COLS, SM_DEV)
    pot_blocks = sample_potential.reshape(N_COLS, SM_DEV)

    def bary_pass(block):
        def piece_pass(triple):
            sblock, sqblock, gblock = triple
            cost = cost_block(block, sblock, sqblock)
            score = (gblock[None, :] - cost) / EPS
            top = jnp.max(score, axis=1)
            weight = jnp.exp(score - top[:, None]).astype(jnp.bfloat16)
            denom = jnp.sum(weight.astype(jnp.float32), axis=1)
            numer = lax.dot_general(sblock, weight, (((1,), (1,)), ((), ())), preferred_element_type=jnp.float32)
            return top, denom, numer

        tops_b, denoms_b, numers_b = lax.map(piece_pass, (sample_blocks, sq_blocks, pot_blocks))
        best_b = jnp.max(tops_b, axis=0)
        scale = jnp.exp(tops_b - best_b[None, :])
        denom = jnp.sum(denoms_b * scale, axis=0)
        numer = jnp.sum(numers_b * scale[:, None, :], axis=0)
        return numer / denom[None, :]

    bary = lax.map(bary_pass, blocks)
    barycenter = bary.transpose(1, 0, 2).reshape(DIM, NPTS)
    return point_potential.reshape(NPTS), sample_potential, barycenter
```

```python
import math

import jax
import jax.numpy as jnp
from jax import lax
from jax.sharding import PartitionSpec as P

EPS = 0.25


def spread(part, axis):
    count = lax.axis_size(axis)
    return lax.all_to_all(jnp.broadcast_to(part, (count,) + part.shape), axis, 0, 0)


def combine(lse):
    top = jnp.max(lse, axis=0)
    return top + jnp.log(jnp.sum(jnp.exp(lse - top[None]), axis=0))


def on_device(points, samples, potential):
    own_count = points.shape[1]
    dim = points.shape[0]
    col_count = lax.axis_size("cols")
    block_count = own_count * col_count
    sample_count = samples.shape[1]
    total_samples = sample_count * col_count
    total_points = block_count * lax.axis_size("rows")
    whole = spread(points.T, "cols").reshape(block_count, dim)
    xf = whole.astype(jnp.float32)
    yf = samples.astype(jnp.float32)
    point_sq = jnp.sum(xf * xf, axis=1)
    sample_sq = jnp.sum(yf * yf, axis=0)
    cross = lax.dot_general(
        whole, samples, (((1,), (0,)), ((), ())), preferred_element_type=jnp.float32
    )
    cost = 0.5 * point_sq[:, None] + 0.5 * sample_sq[None, :] - cross
    score = (potential[None, :] - cost) / EPS
    row_top = jnp.max(score, axis=1)
    row_lse = row_top + jnp.log(jnp.sum(jnp.exp(score - row_top[:, None]), axis=1))
    own_lse = combine(lax.all_to_all(row_lse.reshape(col_count, own_count), "cols", 0, 0))
    point_potential = -EPS * (own_lse - math.log(total_samples))
    point_full = spread(point_potential, "cols").reshape(block_count)
    col_score = (point_full[:, None] - cost) / EPS
    col_top = jnp.max(col_score, axis=0)
    col_lse = col_top + jnp.log(jnp.sum(jnp.exp(col_score - col_top[None, :]), axis=0))
    col_lse = combine(spread(col_lse, "rows"))
    sample_potential = -EPS * (col_lse - math.log(total_points))
    new_score = (sample_potential[None, :] - cost) / EPS
    block_top = jnp.max(new_score, axis=1)
    weight = jnp.exp(new_score - block_top[:, None]).astype(jnp.bfloat16)
    denom = jnp.sum(weight.astype(jnp.float32), axis=1)
    numer = lax.dot_general(
        weight, samples, (((1,), (1,)), ((), ())), preferred_element_type=jnp.float32
    )
    parts = jnp.concatenate([numer, denom[:, None], block_top[:, None]], axis=1)
    parts = parts.reshape(col_count, own_count * (dim + 2))
    parts = lax.all_to_all(parts, "cols", 0, 0).reshape(col_count, own_count, dim + 2)
    top = parts[:, :, dim + 1]
    scale = jnp.exp(top - jnp.max(top, axis=0)[None])
    total = jnp.sum(parts[:, :, : dim + 1] * scale[:, :, None], axis=0)
    barycenter = (total[:, :dim] / total[:, dim:]).T
    return (point_potential, sample_potential, barycenter)


def solution(mesh):
    placed = (P(None, ("rows", "cols")), P(None, "cols"), P("cols"))
    return jax.shard_map(
        on_device,
        mesh=mesh,
        in_specs=placed,
        out_specs=(P(("rows", "cols")), P("cols"), P(None, ("rows", "cols"))),
        check_vma=False,
    )
```

```python
import math

import jax
import jax.numpy as jnp
from jax import lax
from jax.experimental import pallas as pl
from jax.experimental.pallas import tpu as pltpu
from jax.sharding import Mesh, PartitionSpec as P

EPS = 0.25
SCALE = math.log2(math.e) / EPS
MARGIN = 18.0
AXES = ("x_lo", "y", "z", "x_hi", "core")
SHAPE = (2, 4, 16, 2, 2)
PLANE = ("x_lo", "y", "x_hi", "core")
BLOCK = 1024
LANES = 128
F32 = jnp.float32
BF16 = jnp.bfloat16


def row_index():
    return lax.axis_index("x_lo") * 4 + lax.axis_index("y")


def side_index():
    return lax.axis_index("x_hi") * 2 + lax.axis_index("core")


def lanes_of(shape):
    return lax.broadcasted_iota(jnp.int32, shape, len(shape) - 1)


def rows_of(shape):
    return lax.broadcasted_iota(jnp.int32, shape, len(shape) - 2)


def triple(value):
    high = value.astype(BF16).astype(F32)
    rest = value - high
    mid = rest.astype(BF16).astype(F32)
    return high, mid, rest - mid


def place(base, first, values):
    lane = lanes_of(base.shape)
    for step, value in enumerate(values):
        base = jnp.where(lane == first + step, value, base)
    return base


def turned(block):
    rows, cols = block.shape
    if rows < LANES:
        block = jnp.concatenate([block, jnp.zeros((LANES - rows, cols), block.dtype)], axis=0)
    return jnp.transpose(block)


def pair_up(block):
    half = block.shape[0] // 2
    return block[:half] + pltpu.roll(block[half:], 64, 1)


def split_up(packed, groups):
    wide = packed.astype(F32)
    rows = packed.shape[0] // groups
    low = wide.reshape(groups, 1, rows, LANES)
    high = pltpu.roll(wide, 64, 1).reshape(groups, 1, rows, LANES)
    both = jnp.concatenate([low, high], axis=1).reshape(groups * 2 * rows, LANES)
    return jnp.where(lanes_of(both.shape) < 64, both, 0.0)


def product(left, right):
    return lax.dot_general(left, right, (((1,), (1,)), ((), ())), preferred_element_type=F32)


def prepare(points_ref, samples_ref, potential_ref, points_out, samples_out):
    row = row_index()
    x = turned(points_ref[...].astype(F32))
    xp = jnp.concatenate([x, jnp.zeros((32, 96), F32)], axis=1) if x.shape[1] < LANES else x
    half_sq = -0.5 * jnp.sum(xp * xp, axis=1, keepdims=True)
    xp = place(xp, 32, (1.0, 1.0, 1.0) + triple(half_sq))
    points_out[...] = jnp.broadcast_to(pair_up(xp).astype(BF16)[None], (32, 16, LANES))
    start = pl.multiple_of(row // 2 * LANES, LANES)
    y = turned(samples_ref[:, pl.ds(start, LANES)].astype(F32))
    line = potential_ref[pl.ds(row // 2, 1), :]
    pot = jnp.transpose(jnp.broadcast_to(line, (LANES, LANES)))
    odd = row % 2 == 1
    y = jnp.where(odd, y[64:], y[:64])
    pot = jnp.where(odd, pot[64:], pot[:64])
    half_sq = -0.5 * jnp.sum(y * y, axis=1, keepdims=True)
    y = place(y, 32, triple(half_sq) + (1.0, 1.0, 1.0) + triple(pot) + (1.0, 1.0, 1.0))
    samples_out[...] = jnp.broadcast_to(pair_up(y).astype(BF16)[None], (16, 32, LANES))


def row_pass(points_ref, samples_ref, x_out, y_out, lse_out):
    x = split_up(points_ref[...], 32)
    packed = samples_ref[...].astype(F32)
    lane = lanes_of(packed.shape) % 64
    shift = jnp.max(jnp.where(lane == 38, packed, -1e30)) - MARGIN
    y = split_up(samples_ref[...], 16).astype(BF16)
    x_out[...] = x.astype(BF16)
    y_out[...] = y
    x = place(x, 38, (1.0, 1.0, 1.0) + triple(jnp.full((1, 1), -shift, F32))).astype(BF16)
    lse = jnp.zeros((8, LANES), F32)
    for tile in range(8):
        total = jnp.zeros((8, LANES), F32)
        for chunk in range(4):
            part = product(y[chunk * 256 : chunk * 256 + 256], x[tile * 128 : tile * 128 + 128])
            total += jnp.sum(jnp.exp2(part * SCALE).reshape(32, 8, LANES), axis=0)
        line = jnp.log2(jnp.sum(total, axis=0, keepdims=True)) + SCALE * shift
        lse = jnp.where(rows_of(lse.shape) == tile, line, lse)
    lse_out[...] = jnp.broadcast_to(lse[None], (32, 8, LANES))


def combine(lse):
    top = jnp.max(lse, axis=0)
    return top + jnp.log2(jnp.sum(jnp.exp2(lse - top[None]), axis=0))


def columns(block):
    flipped = turned(block)
    return jnp.concatenate(
        [jnp.broadcast_to(flipped[:, k : k + 1], (LANES, LANES)) for k in range(8)], axis=0
    )


def col_pass(x_ref, y_ref, rows_ref, lse_out, point_out, own_out):
    log_samples = math.log2(BLOCK * 32)
    point = log_samples - combine(rows_ref[...])
    point_out[...] = point
    me = row_index() * 4 + side_index()
    line = jnp.sum(jnp.where(rows_of(point.shape) == me // 4, point, 0.0), axis=0, keepdims=True)
    line = pltpu.roll(jnp.broadcast_to(line, (8, LANES)), (4 - me % 4) * 32 % LANES, 1)
    own_out[...] = line[:1, :32] / SCALE
    shift = jnp.max(point) - MARGIN * SCALE
    column = columns(point - shift)
    lse = jnp.zeros((8, LANES), F32)
    for tile in range(8):
        total = jnp.zeros((8, LANES), F32)
        y = y_ref[tile * 128 : tile * 128 + 128, :]
        for chunk in range(4):
            part = product(x_ref[chunk * 256 : chunk * 256 + 256, :], y)
            part = part * SCALE + column[chunk * 256 : chunk * 256 + 256]
            total += jnp.sum(jnp.exp2(part).reshape(32, 8, LANES), axis=0)
        line = jnp.log2(jnp.sum(total, axis=0, keepdims=True)) + shift
        lse = jnp.where(rows_of(lse.shape) == tile, line, lse)
    lse_out[...] = jnp.broadcast_to(lse[None], (16, 8, LANES))


def weigh(x_ref, y_ref, point_ref, cols_ref, parts_out):
    log_points = math.log2(BLOCK * 16)
    sample = log_points - combine(cols_ref[...])
    z = lax.axis_index("z")
    line = jnp.sum(jnp.where(rows_of(sample.shape) == z // 2, sample, 0.0), axis=0, keepdims=True)
    line = jnp.broadcast_to(line, (8, LANES)) / SCALE
    line = jnp.where(z % 2 == 1, line, pltpu.roll(line, 64, 1))
    column = columns(point_ref[...])
    y = y_ref[...]
    wide = jnp.where(lanes_of(y.shape) < 32, y.astype(F32), 0.0)
    wide = wide + pltpu.roll(wide, 32, 1)
    wide = wide + pltpu.roll(wide, 64, 1)
    right = jnp.concatenate([wide.astype(BF16), jnp.ones((BLOCK, LANES), BF16)], axis=1)
    lane = lanes_of((4, 8, LANES))
    for tile in range(8):
        x = x_ref[tile * 128 : tile * 128 + 128, :]
        total = jnp.zeros((LANES, 2 * LANES), F32)
        for chunk in range(4):
            rows = slice(chunk * 256, chunk * 256 + 256)
            part = product(x, y[rows]) * SCALE
            both = jnp.concatenate([sample[2 * chunk : 2 * chunk + 1], sample[2 * chunk + 1 : 2 * chunk + 2]], axis=1)
            one = column[tile * 128 : tile * 128 + 128]
            part = part + jnp.concatenate([one, one], axis=1) + both
            weight = jnp.exp2(part).astype(BF16)
            total += jnp.dot(weight, right[rows], preferred_element_type=F32)
        numer = total[:, :LANES].reshape(4, 4, 8, LANES)
        denom = total[:, LANES:].reshape(4, 4, 8, LANES)
        first = numer[:, 0]
        second = denom[:, 0]
        for q in range(1, 4):
            first = jnp.where(lane // 32 == q, numer[:, q], first)
            second = jnp.where(lane // 16 == q, denom[:, q], second)
        second = jnp.where(lane >= 64, line[None], second)
        parts_out[tile * 4 : tile * 4 + 4, :8, :] = first
        parts_out[tile * 4 : tile * 4 + 4, 8:, :] = second


def finish(parts_ref, bary_out, sample_out):
    total = jnp.sum(parts_ref[...], axis=0)
    numer, denom = total[:8], total[8:]
    lane = lanes_of((8, LANES))
    below = jnp.broadcast_to(denom[:, :1], (8, LANES))
    for q in range(1, 4):
        below = jnp.where(lane // 32 == q, jnp.broadcast_to(denom[:, 16 * q : 16 * q + 1], (8, LANES)), below)
    ratio = numer / below
    stack = jnp.concatenate([ratio] + [pltpu.roll(ratio, LANES - 32 * q, 1) for q in range(1, 4)], axis=0)
    bary_out[...] = turned(stack)[:32, :32]
    side = side_index()
    lines = []
    for pair in range(4):
        even = parts_ref[pl.ds(8 * pair + side, 1), 8:, :][0]
        odd = parts_ref[pl.ds(8 * pair + 4 + side, 1), 8:, :][0]
        lines.append(jnp.where(lane < 64, pltpu.roll(even, 64, 1), odd)[:1])
    sample_out[...] = jnp.concatenate(lines, axis=0)


def call(body, outs, *args):
    vmem = pl.BlockSpec(memory_space=pltpu.VMEM)
    return pl.pallas_call(
        body,
        out_shape=[jax.ShapeDtypeStruct(shape, dtype) for shape, dtype in outs],
        in_specs=[vmem] * len(args),
        out_specs=[vmem] * len(outs),
    )(*args)


def on_device(points, samples, potential):
    xs, ys = call(
        prepare,
        [((32, 16, LANES), BF16), ((16, 32, LANES), BF16)],
        points, samples, potential.reshape(4, LANES),
    )
    xs = lax.all_to_all(xs, PLANE, 0, 0).reshape(512, LANES)
    ys = lax.all_to_all(ys, "z", 0, 0).reshape(512, LANES)
    x, y, rows = call(
        row_pass,
        [((BLOCK, LANES), BF16), ((BLOCK, LANES), BF16), ((32, 8, LANES), F32)],
        xs, ys,
    )
    rows = lax.all_to_all(rows, PLANE, 0, 0)
    cols, point, own = call(
        col_pass,
        [((16, 8, LANES), F32), ((8, LANES), F32), ((1, 32), F32)],
        x, y, rows,
    )
    cols = lax.all_to_all(cols, "z", 0, 0)
    (parts,) = call(weigh, [((32, 16, LANES), F32)], x, y, point, cols)
    parts = lax.all_to_all(parts, PLANE, 0, 0)
    bary, sample = call(finish, [((32, 32), F32), ((4, LANES), F32)], parts)
    return own.reshape(32), sample.reshape(512), bary


def solution(mesh):
    split = Mesh(mesh.devices.reshape(SHAPE), AXES)
    return jax.shard_map(
        on_device,
        mesh=split,
        in_specs=(P(None, AXES), P(None, ("z", "x_hi", "core")), P(("z", "x_hi", "core"))),
        out_specs=(P(AXES), P(("z", "x_hi", "core")), P(None, AXES)),
        check_vma=False,
    )
```

```python
import math

import jax
import jax.numpy as jnp
from jax import lax
from jax.experimental import pallas as pl
from jax.experimental.pallas import tpu as pltpu
from jax.sharding import Mesh, PartitionSpec as P

EPS = 0.25
SCALE = math.log2(math.e) / EPS
MARGIN = 18.0
AXES = ("x_lo", "y", "z", "x_hi", "core")
SHAPE = (2, 4, 16, 2, 2)
PLANE = ("x_lo", "y", "x_hi", "core")
POINTS = 512
SAMPLES = 2048
LOG_POINTS = math.log2(POINTS * 32)
LOG_SAMPLES = math.log2(SAMPLES * 16)
LANES = 128
DEPTH = 48
F32 = jnp.float32
BF16 = jnp.bfloat16


def lanes_of(shape):
    return lax.broadcasted_iota(jnp.int32, shape, len(shape) - 1)


def rows_of(shape):
    return lax.broadcasted_iota(jnp.int32, shape, len(shape) - 2)


def triple(value):
    high = value.astype(BF16).astype(F32)
    rest = value - high
    mid = rest.astype(BF16).astype(F32)
    return high, mid, rest - mid


def turned(block):
    rows, cols = block.shape
    if rows < LANES:
        block = jnp.concatenate([block, jnp.zeros((LANES - rows, cols), block.dtype)], axis=0)
    return jnp.transpose(block)


def combine(lse):
    top = jnp.max(lse, axis=0)
    return top + jnp.log2(jnp.sum(jnp.exp2(lse - top[None]), axis=0))


def line_up(block):
    return jnp.concatenate([block[k : k + 1] for k in range(block.shape[0])], axis=1)


def stack_up(lines):
    lane = rows_of((len(lines), LANES))
    block = jnp.broadcast_to(lines[0], lane.shape)
    for k, line in enumerate(lines[1:], 1):
        block = jnp.where(lane == k, line, block)
    return block


def extra_rows(value):
    row = rows_of((16, value.shape[1]))
    block = jnp.where((row >= 3) & (row < 9), 1.0, 0.0)
    for k, part in enumerate(triple(value)):
        block = jnp.where(row == k, part, block)
    return block.astype(BF16)


def prepare_points(points_ref, points_out):
    x = turned(points_ref[...].astype(F32))
    packed = x[:8]
    for q in range(1, 4):
        packed = packed + pltpu.roll(x[8 * q : 8 * q + 8], 32 * q, 1)
    points_out[...] = jnp.broadcast_to(packed.astype(BF16)[None], (16, 8, LANES))


def prepare_samples(samples_ref, potential_ref, samples_out):
    samples_out[:32, :] = samples_ref[...]
    pot = potential_ref[...]
    row = rows_of((8, 512))
    block = jnp.zeros((8, 512), F32)
    for k, part in enumerate(triple(pot)):
        block = jnp.where(row == k, part, block)
    samples_out[32:, :] = block.astype(BF16)


def row_pass(points_ref, own_ref, core_ref, side_ref, both_ref, x_out, y_out, lse_out):
    packed = points_ref[...].astype(F32)
    x = jnp.concatenate(
        [packed.reshape(16, 1, 8, LANES)]
        + [pltpu.roll(packed, LANES - 32 * q, 1).reshape(16, 1, 8, LANES) for q in range(1, 4)],
        axis=1,
    ).reshape(POINTS, LANES)
    lane = lanes_of(x.shape)
    x = jnp.where(lane < 32, x, 0.0)
    x_norm = -0.5 * jnp.sum(x * x, axis=1, keepdims=True)
    x = jnp.where((lane >= 32) & (lane < 35), 1.0, x)
    for k, part in enumerate(triple(x_norm)):
        x = jnp.where(lane == 35 + k, part, x)
    x = x[:, :DEPTH].astype(BF16)
    x_out[...] = x
    side = lax.axis_index("x_hi") == 1
    core = lax.axis_index("core") == 1
    blocks = [ref[...].astype(F32) for ref in (own_ref, core_ref, side_ref, both_ref)]
    swap = [blocks[1], blocks[0], blocks[3], blocks[2]]
    blocks = [jnp.where(core, b, a) for a, b in zip(blocks, swap)]
    swap = blocks[2:] + blocks[:2]
    y = jnp.concatenate([jnp.where(side, b, a) for a, b in zip(blocks, swap)], axis=1)
    pot = jnp.sum(y[32:40], axis=0, keepdims=True)
    y = y[:32]
    y_norm = -0.5 * jnp.sum(y * y, axis=0, keepdims=True)
    shift = jnp.max(pot) - MARGIN
    y_out[:32, :] = y.astype(BF16)
    y_out[32:, :] = extra_rows(y_norm)
    y = jnp.concatenate([y.astype(BF16), extra_rows(y_norm + pot - shift)], axis=0)
    lines = []
    for tile in range(4):
        total = jnp.zeros((LANES, LANES), F32)
        left = x[tile * 128 : tile * 128 + 128]
        for chunk in range(8):
            right = y[:, chunk * 256 : chunk * 256 + 256]
            part = jnp.exp2(jnp.dot(left, right, preferred_element_type=F32) * SCALE)
            total += part[:, :LANES] + part[:, LANES:]
        total = jnp.sum(jnp.transpose(total), axis=0, keepdims=True)
        lines.append(jnp.log2(total) + SCALE * shift)
    lse_out[...] = jnp.broadcast_to(stack_up(lines)[None], (16, 4, LANES))


def col_pass(x_ref, y_ref, rows_ref, x_out, shift_out, lse_out, own_out):
    point = (LOG_SAMPLES - combine(rows_ref[...])) / SCALE
    z = lax.axis_index("z")
    line = jnp.sum(jnp.where(rows_of(point.shape) == z // 4, point, 0.0), axis=0, keepdims=True)
    line = pltpu.roll(jnp.broadcast_to(line, (8, LANES)), (4 - z % 4) * 32 % LANES, 1)
    own_out[...] = line[:1, :32]
    shift = jnp.max(point) - MARGIN
    shift_out[...] = jnp.full((1, LANES), shift, F32)
    flipped = turned(point - shift)
    x = x_ref[...].astype(F32)
    column = jnp.concatenate([flipped[:, k : k + 1] for k in range(4)], axis=0)
    lane = lanes_of(x.shape)
    for k, part in enumerate(triple(column)):
        x = jnp.where(lane == 38 + k, part, x)
    x = x.astype(BF16)
    x_out[...] = x
    lines = []
    for chunk in range(8):
        total = jnp.zeros((8, 256), F32)
        right = y_ref[:, chunk * 256 : chunk * 256 + 256]
        for tile in range(4):
            left = x[tile * 128 : tile * 128 + 128]
            part = jnp.exp2(jnp.dot(left, right, preferred_element_type=F32) * SCALE)
            total += jnp.sum(part.reshape(16, 8, 256), axis=0)
        total = jnp.log2(jnp.sum(total, axis=0, keepdims=True)) + SCALE * shift
        lines += [total[:, :LANES], total[:, LANES:]]
    lse_out[...] = jnp.broadcast_to(stack_up(lines)[None], (32, 16, LANES))


def weigh(x_ref, y_ref, shift_ref, cols_ref, parts_out, sample_out):
    sample = (LOG_POINTS - combine(cols_ref[...])) / SCALE
    side = lax.axis_index("x_hi") * 2 + lax.axis_index("core")
    own = sample[:4]
    for k in range(1, 4):
        own = jnp.where(side == k, sample[4 * k : 4 * k + 4], own)
    sample_out[...] = own
    y = y_ref[:32, :]
    y_norm = jnp.sum(y_ref[32:, :].astype(F32)[:3], axis=0, keepdims=True)
    shift = jnp.max(shift_ref[...])
    y_all = jnp.concatenate([y, extra_rows(y_norm + line_up(sample) + shift)], axis=0)
    right = jnp.concatenate([y, y, y, y, jnp.ones((LANES, SAMPLES), BF16)], axis=0)
    lane = lanes_of((4, 8, LANES))
    for tile in range(4):
        x = x_ref[tile * 128 : tile * 128 + 128, :]
        total = jnp.zeros((LANES, 2 * LANES), F32)
        for chunk in range(8):
            cols = slice(chunk * 256, chunk * 256 + 256)
            weight = jnp.exp2(jnp.dot(x, y_all[:, cols], preferred_element_type=F32) * SCALE)
            total += lax.dot_general(
                weight.astype(BF16),
                right[:, cols],
                (((1,), (1,)), ((), ())),
                preferred_element_type=F32,
            )
        numer = total[:, :LANES].reshape(4, 4, 8, LANES)
        denom = total[:, LANES:].reshape(4, 4, 8, LANES)
        first, second = numer[:, 0], denom[:, 0]
        for q in range(1, 4):
            first = jnp.where(lane // 32 == q, numer[:, q], first)
            second = jnp.where(lane // 32 == q, denom[:, q], second)
        parts_out[tile * 4 : tile * 4 + 4, :8, :] = first
        parts_out[tile * 4 : tile * 4 + 4, 8:, :] = second


def finish(parts_ref, bary_out):
    total = jnp.sum(parts_ref[...], axis=0)
    ratio = total[:8] / total[8:]
    stack = jnp.concatenate([ratio] + [pltpu.roll(ratio, LANES - 32 * q, 1) for q in range(1, 4)], axis=0)
    bary_out[...] = turned(stack)[:32, :32]


def call(body, outs, *args):
    vmem = pl.BlockSpec(memory_space=pltpu.VMEM)
    return pl.pallas_call(
        body,
        out_shape=[jax.ShapeDtypeStruct(shape, dtype) for shape, dtype in outs],
        in_specs=[vmem] * len(args),
        out_specs=[vmem] * len(outs),
        compiler_params=pltpu.CompilerParams(vmem_limit_bytes=8 << 20),
    )(*args)


def on_device(points, samples, potential):
    (xs,) = call(prepare_points, [((16, 8, LANES), BF16)], points)
    xs = lax.all_to_all(xs, "z", 0, 0).reshape(LANES, LANES)
    (own,) = call(prepare_samples, [((40, 512), BF16)], samples, potential.reshape(1, 512))
    core = lax.ppermute(own, "core", [(0, 1), (1, 0)])
    side = lax.ppermute(own, "x_hi", [(0, 1), (1, 0)])
    both = lax.ppermute(own, ("x_hi", "core"), [(k, 3 - k) for k in range(4)])
    x, y, rows = call(
        row_pass,
        [((POINTS, DEPTH), BF16), ((DEPTH, SAMPLES), BF16), ((16, 4, LANES), F32)],
        xs, own, core, side, both,
    )
    rows = lax.all_to_all(rows, "z", 0, 0)
    x, shift, cols, point = call(
        col_pass,
        [((POINTS, DEPTH), BF16), ((1, LANES), F32), ((32, 16, LANES), F32), ((1, 32), F32)],
        x, y, rows,
    )
    cols = lax.all_to_all(cols, PLANE, 0, 0)
    parts, sample = call(
        weigh, [((16, 16, LANES), F32), ((4, LANES), F32)], x, y, shift, cols
    )
    parts = lax.all_to_all(parts, "z", 0, 0)
    (bary,) = call(finish, [((32, 32), F32)], parts)
    return point.reshape(32), sample.reshape(512), bary


def solution(mesh):
    split = Mesh(mesh.devices.reshape(SHAPE), AXES)
    cols = ("z", "x_hi", "core")
    return jax.shard_map(
        on_device,
        mesh=split,
        in_specs=(P(None, AXES), P(None, cols), P(cols)),
        out_specs=(P(AXES), P(cols), P(None, AXES)),
        check_vma=False,
    )
```

```python
import math

import jax
import jax.numpy as jnp
from jax import lax
from jax.experimental import pallas as pl
from jax.experimental.pallas import tpu as pltpu
from jax.sharding import Mesh, PartitionSpec as P

EPS = 0.25
SCALE = math.log2(math.e) / EPS
MARGIN = 18.0
AXES = ("x_lo", "y", "z", "x_hi", "core")
SHAPE = (2, 4, 16, 2, 2)
PLANE = ("x_lo", "y", "x_hi", "core")
POINTS = 512
SAMPLES = 2048
LOG_POINTS = math.log2(POINTS * 32)
LOG_SAMPLES = math.log2(SAMPLES * 16)
LANES = 128
DEPTH = 48
F32 = jnp.float32
BF16 = jnp.bfloat16


def lanes_of(shape):
    return lax.broadcasted_iota(jnp.int32, shape, len(shape) - 1)


def rows_of(shape):
    return lax.broadcasted_iota(jnp.int32, shape, len(shape) - 2)


def triple(value):
    high = value.astype(BF16).astype(F32)
    rest = value - high
    mid = rest.astype(BF16).astype(F32)
    return high, mid, rest - mid


def turned(block):
    rows, cols = block.shape
    if rows < LANES:
        block = jnp.concatenate([block, jnp.zeros((LANES - rows, cols), block.dtype)], axis=0)
    return jnp.transpose(block)


def combine(lse):
    top = jnp.max(lse, axis=0)
    return top + jnp.log2(jnp.sum(jnp.exp2(lse - top[None]), axis=0))


def line_up(block):
    return jnp.concatenate([block[k : k + 1] for k in range(block.shape[0])], axis=1)


def stack_up(lines):
    lane = rows_of((len(lines), LANES))
    block = jnp.broadcast_to(lines[0], lane.shape)
    for k, line in enumerate(lines[1:], 1):
        block = jnp.where(lane == k, line, block)
    return block


def extra_rows(value):
    row = rows_of((16, value.shape[1]))
    block = jnp.where((row >= 3) & (row < 9), 1.0, 0.0)
    for k, part in enumerate(triple(value)):
        block = jnp.where(row == k, part, block)
    return block.astype(BF16)


def prepare_points(points_ref, points_out):
    x = turned(points_ref[...].astype(F32))
    packed = x[:8]
    for q in range(1, 4):
        packed = packed + pltpu.roll(x[8 * q : 8 * q + 8], 32 * q, 1)
    points_out[...] = jnp.broadcast_to(packed.astype(BF16)[None], (16, 8, LANES))


def prepare_samples(samples_ref, potential_ref, samples_out):
    samples_out[:32, :] = samples_ref[...]
    pot = potential_ref[...]
    row = rows_of((8, 512))
    block = jnp.zeros((8, 512), F32)
    for k, part in enumerate(triple(pot)):
        block = jnp.where(row == k, part, block)
    samples_out[32:, :] = block.astype(BF16)


def row_pass(points_ref, samples_ref, x_out, y_out, lse_out):
    packed = points_ref[...].astype(F32)
    x = jnp.concatenate(
        [packed.reshape(16, 1, 8, LANES)]
        + [pltpu.roll(packed, LANES - 32 * q, 1).reshape(16, 1, 8, LANES) for q in range(1, 4)],
        axis=1,
    ).reshape(POINTS, LANES)
    lane = lanes_of(x.shape)
    x = jnp.where(lane < 32, x, 0.0)
    x_norm = -0.5 * jnp.sum(x * x, axis=1, keepdims=True)
    x = jnp.where((lane >= 32) & (lane < 35), 1.0, x)
    for k, part in enumerate(triple(x_norm)):
        x = jnp.where(lane == 35 + k, part, x)
    x = x[:, :DEPTH].astype(BF16)
    x_out[...] = x
    y = jnp.concatenate([samples_ref[k].astype(F32) for k in range(4)], axis=1)
    pot = jnp.sum(y[32:40], axis=0, keepdims=True)
    y = y[:32]
    y_norm = -0.5 * jnp.sum(y * y, axis=0, keepdims=True)
    shift = jnp.max(pot) - MARGIN
    y_out[:32, :] = y.astype(BF16)
    y_out[32:, :] = extra_rows(y_norm)
    y = jnp.concatenate([y.astype(BF16), extra_rows(y_norm + pot - shift)], axis=0)
    total = jnp.zeros((POINTS, LANES), F32)
    for chunk in range(8):
        right = y[:, chunk * 256 : chunk * 256 + 256]
        part = jnp.exp2(jnp.dot(x, right, preferred_element_type=F32) * SCALE)
        total += part[:, :LANES] + part[:, LANES:]
    lines = []
    for tile in range(4):
        line = jnp.transpose(total[tile * 128 : tile * 128 + 128])
        line = jnp.sum(line, axis=0, keepdims=True)
        lines.append(jnp.log2(line) + SCALE * shift)
    lse_out[...] = jnp.broadcast_to(stack_up(lines)[None], (16, 4, LANES))


def col_pass(x_ref, y_ref, rows_ref, x_out, shift_out, lse_out, own_out):
    point = (LOG_SAMPLES - combine(rows_ref[...])) / SCALE
    z = lax.axis_index("z")
    line = jnp.sum(jnp.where(rows_of(point.shape) == z // 4, point, 0.0), axis=0, keepdims=True)
    line = pltpu.roll(jnp.broadcast_to(line, (8, LANES)), (4 - z % 4) * 32 % LANES, 1)
    own_out[...] = line[:1, :32]
    shift = jnp.max(point) - MARGIN
    shift_out[...] = jnp.full((1, LANES), shift, F32)
    flipped = turned(point - shift)
    x = x_ref[...].astype(F32)
    column = jnp.concatenate([flipped[:, k : k + 1] for k in range(4)], axis=0)
    lane = lanes_of(x.shape)
    for k, part in enumerate(triple(column)):
        x = jnp.where(lane == 38 + k, part, x)
    x = x.astype(BF16)
    x_out[...] = x
    lines = []
    for chunk in range(8):
        right = y_ref[:, chunk * 256 : chunk * 256 + 256]
        part = jnp.exp2(jnp.dot(x, right, preferred_element_type=F32) * SCALE)
        total = jnp.sum(part.reshape(64, 8, 256), axis=0)
        total = jnp.log2(jnp.sum(total, axis=0, keepdims=True)) + SCALE * shift
        lines += [total[:, :LANES], total[:, LANES:]]
    lse_out[...] = jnp.broadcast_to(stack_up(lines)[None], (32, 16, LANES))


def weigh(x_ref, y_ref, shift_ref, cols_ref, parts_out, sample_out):
    sample = (LOG_POINTS - combine(cols_ref[...])) / SCALE
    side = lax.axis_index("x_hi") * 2 + lax.axis_index("core")
    own = sample[:4]
    for k in range(1, 4):
        own = jnp.where(side == k, sample[4 * k : 4 * k + 4], own)
    sample_out[...] = own
    y = y_ref[:32, :]
    y_norm = jnp.sum(y_ref[32:, :].astype(F32)[:3], axis=0, keepdims=True)
    shift = jnp.max(shift_ref[...])
    y_all = jnp.concatenate([y, extra_rows(y_norm + line_up(sample) + shift)], axis=0)
    right = jnp.concatenate([y, y, y, y, jnp.ones((LANES, SAMPLES), BF16)], axis=0)
    x = x_ref[...]
    total = jnp.zeros((POINTS, 2 * LANES), F32)
    for chunk in range(8):
        cols = slice(chunk * 256, chunk * 256 + 256)
        weight = jnp.exp2(jnp.dot(x, y_all[:, cols], preferred_element_type=F32) * SCALE)
        total += lax.dot_general(
            weight.astype(BF16),
            right[:, cols],
            (((1,), (1,)), ((), ())),
            preferred_element_type=F32,
        )
    numer = total[:, :LANES].reshape(16, 4, 8, LANES)
    denom = total[:, LANES:].reshape(16, 4, 8, LANES)
    shape = (16, 8, LANES)
    lane, row = lanes_of(shape), rows_of(shape)
    first, second = numer[:, 0], jnp.where(lane == row, denom[:, 0], 0.0)
    for q in range(1, 4):
        first = jnp.where(lane // 32 == q, numer[:, q], first)
        second = jnp.where(lane == row + 8 * q, denom[:, q], second)
    second = jnp.sum(second, axis=1)
    for peer in range(16):
        parts_out[9 * peer : 9 * peer + 8, :] = first[peer]
        parts_out[9 * peer + 8 : 9 * peer + 9, :] = second[peer : peer + 1]


def finish(parts_ref, bary_out):
    numer, denom = parts_ref[:8, :], parts_ref[8:9, :]
    for peer in range(1, 16):
        numer = numer + parts_ref[9 * peer : 9 * peer + 8, :]
        denom = denom + parts_ref[9 * peer + 8 : 9 * peer + 9, :]
    stack = [numer] + [pltpu.roll(numer, LANES - 32 * q, 1) for q in range(1, 4)]
    bary_out[...] = turned(jnp.concatenate(stack, axis=0))[:32, :32] / denom[:, :32]


def call(body, outs, *args):
    vmem = pl.BlockSpec(memory_space=pltpu.VMEM)
    return pl.pallas_call(
        body,
        out_shape=[jax.ShapeDtypeStruct(shape, dtype) for shape, dtype in outs],
        in_specs=[vmem] * len(args),
        out_specs=[vmem] * len(outs),
        compiler_params=pltpu.CompilerParams(vmem_limit_bytes=8 << 20),
    )(*args)


def on_device(points, samples, potential):
    (xs,) = call(prepare_points, [((16, 8, LANES), BF16)], points)
    xs = lax.all_to_all(xs, "z", 0, 0).reshape(LANES, LANES)
    (own,) = call(prepare_samples, [((40, 512), BF16)], samples, potential.reshape(1, 512))
    ys = lax.all_gather(own, ("x_hi", "core"))
    x, y, rows = call(
        row_pass,
        [((POINTS, DEPTH), BF16), ((DEPTH, SAMPLES), BF16), ((16, 4, LANES), F32)],
        xs, ys,
    )
    rows = lax.all_to_all(rows, "z", 0, 0)
    x, shift, cols, point = call(
        col_pass,
        [((POINTS, DEPTH), BF16), ((1, LANES), F32), ((32, 16, LANES), F32), ((1, 32), F32)],
        x, y, rows,
    )
    cols = lax.all_to_all(cols, PLANE, 0, 0)
    parts, sample = call(
        weigh, [((144, LANES), F32), ((4, LANES), F32)], x, y, shift, cols
    )
    parts = parts.reshape(16, 9, 1, LANES)
    parts = lax.all_to_all(parts, "z", 0, 0).reshape(144, LANES)
    (bary,) = call(finish, [((32, 32), F32)], parts)
    return point.reshape(32), sample.reshape(512), bary


def solution(mesh):
    split = Mesh(mesh.devices.reshape(SHAPE), AXES)
    cols = ("z", "x_hi", "core")
    return jax.shard_map(
        on_device,
        mesh=split,
        in_specs=(P(None, AXES), P(None, cols), P(cols)),
        out_specs=(P(AXES), P(cols), P(None, AXES)),
        check_vma=False,
    )
```

```python
import math

import jax
import jax.numpy as jnp
from jax import lax
from jax.experimental import pallas as pl
from jax.experimental.pallas import tpu as pltpu
from jax.sharding import Mesh, PartitionSpec as P

EPS = 0.25
SCALE = math.log2(math.e) / EPS
MARGIN = 18.0
AXES = ("x_lo", "y", "z", "x_hi", "core")
SHAPE = (2, 4, 16, 2, 2)
PLANE = ("x_lo", "y", "x_hi", "core")
POINTS = 512
SAMPLES = 2048
LOG_POINTS = math.log2(POINTS * 32)
LOG_SAMPLES = math.log2(SAMPLES * 16)
LANES = 128
DEPTH = 48
F32 = jnp.float32
BF16 = jnp.bfloat16


def lanes_of(shape):
    return lax.broadcasted_iota(jnp.int32, shape, len(shape) - 1)


def rows_of(shape):
    return lax.broadcasted_iota(jnp.int32, shape, len(shape) - 2)


def triple(value):
    high = value.astype(BF16).astype(F32)
    rest = value - high
    mid = rest.astype(BF16).astype(F32)
    return high, mid, rest - mid


def turned(block):
    rows, cols = block.shape
    if rows < LANES:
        block = jnp.concatenate([block, jnp.zeros((LANES - rows, cols), block.dtype)], axis=0)
    return jnp.transpose(block)


def combine(lse):
    top = jnp.max(lse, axis=0)
    return top + jnp.log2(jnp.sum(jnp.exp2(lse - top[None]), axis=0))


def line_up(block):
    return jnp.concatenate([block[k : k + 1] for k in range(block.shape[0])], axis=1)


def stack_up(lines):
    lane = rows_of((len(lines), LANES))
    block = jnp.broadcast_to(lines[0], lane.shape)
    for k, line in enumerate(lines[1:], 1):
        block = jnp.where(lane == k, line, block)
    return block


def extra_rows(value):
    row = rows_of((16, value.shape[1]))
    block = jnp.where((row >= 3) & (row < 9), 1.0, 0.0)
    for k, part in enumerate(triple(value)):
        block = jnp.where(row == k, part, block)
    return block.astype(BF16)


def prepare_points(points_ref, points_out):
    x = turned(points_ref[...].astype(F32))
    packed = x[:8]
    for q in range(1, 4):
        packed = packed + pltpu.roll(x[8 * q : 8 * q + 8], 32 * q, 1)
    points_out[...] = jnp.broadcast_to(packed.astype(BF16)[None], (16, 8, LANES))


def prepare_samples(samples_ref, potential_ref, samples_out):
    samples_out[:32, :] = samples_ref[...]
    pot = potential_ref[...]
    row = rows_of((8, 512))
    block = jnp.zeros((8, 512), F32)
    for k, part in enumerate(triple(pot)):
        block = jnp.where(row == k, part, block)
    samples_out[32:, :] = block.astype(BF16)


def row_pass(points_ref, samples_ref, x_out, y_out, lse_out):
    packed = points_ref[...].astype(F32)
    x = jnp.concatenate(
        [packed.reshape(16, 1, 8, LANES)]
        + [pltpu.roll(packed, LANES - 32 * q, 1).reshape(16, 1, 8, LANES) for q in range(1, 4)],
        axis=1,
    ).reshape(POINTS, LANES)
    lane = lanes_of(x.shape)
    x = jnp.where(lane < 32, x, 0.0)
    x_norm = -0.5 * jnp.sum(x * x, axis=1, keepdims=True)
    x = jnp.where((lane >= 32) & (lane < 35), 1.0, x)
    for k, part in enumerate(triple(x_norm)):
        x = jnp.where(lane == 35 + k, part, x)
    x = x[:, :DEPTH].astype(BF16)
    x_out[...] = x
    y = jnp.concatenate([samples_ref[k].astype(F32) for k in range(4)], axis=1)
    pot = jnp.sum(y[32:40], axis=0, keepdims=True)
    y = y[:32]
    y_norm = -0.5 * jnp.sum(y * y, axis=0, keepdims=True)
    shift = jnp.max(pot) - MARGIN
    y_out[:32, :] = y.astype(BF16)
    y_out[32:, :] = extra_rows(y_norm)
    y = jnp.concatenate([y.astype(BF16), extra_rows(y_norm + pot - shift)], axis=0)
    total = jnp.zeros((POINTS, LANES), F32)
    for chunk in range(8):
        right = y[:, chunk * 256 : chunk * 256 + 256]
        part = jnp.exp2(jnp.dot(x, right, preferred_element_type=F32) * SCALE)
        total += part[:, :LANES] + part[:, LANES:]
    lines = []
    for tile in range(4):
        line = jnp.transpose(total[tile * 128 : tile * 128 + 128])
        line = jnp.sum(line, axis=0, keepdims=True)
        lines.append(jnp.log2(line) + SCALE * shift)
    lse_out[...] = jnp.broadcast_to(stack_up(lines)[None], (16, 4, LANES))


def col_pass(x_ref, y_ref, rows_ref, x_out, shift_out, lse_out, own_out):
    point = (LOG_SAMPLES - combine(rows_ref[...])) / SCALE
    z = (lax.axis_index("z") + 6) % 16
    line = jnp.sum(jnp.where(rows_of(point.shape) == z // 4, point, 0.0), axis=0, keepdims=True)
    line = pltpu.roll(jnp.broadcast_to(line, (8, LANES)), (4 - z % 4) * 32 % LANES, 1)
    own_out[...] = line[:1, :32]
    shift = jnp.max(point) - MARGIN
    shift_out[...] = jnp.full((1, LANES), shift, F32)
    flipped = turned(point - shift)
    x = x_ref[...].astype(F32)
    column = jnp.concatenate([flipped[:, k : k + 1] for k in range(4)], axis=0)
    lane = lanes_of(x.shape)
    for k, part in enumerate(triple(column)):
        x = jnp.where(lane == 38 + k, part, x)
    x = x.astype(BF16)
    x_out[...] = x
    lines = []
    for chunk in range(8):
        right = y_ref[:, chunk * 256 : chunk * 256 + 256]
        part = jnp.exp2(jnp.dot(x, right, preferred_element_type=F32) * SCALE)
        total = jnp.sum(part.reshape(64, 8, 256), axis=0)
        total = jnp.log2(jnp.sum(total, axis=0, keepdims=True)) + SCALE * shift
        lines += [total[:, :LANES], total[:, LANES:]]
    lse_out[...] = jnp.broadcast_to(stack_up(lines)[None], (32, 16, LANES))


def weigh(x_ref, y_ref, shift_ref, cols_ref, parts_out, sample_out):
    sample = (LOG_POINTS - combine(cols_ref[...])) / SCALE
    side = lax.axis_index("x_hi") * 2 + lax.axis_index("core")
    own = sample[:4]
    for k in range(1, 4):
        own = jnp.where(side == k, sample[4 * k : 4 * k + 4], own)
    sample_out[...] = own
    y = y_ref[:32, :]
    y_norm = jnp.sum(y_ref[32:, :].astype(F32)[:3], axis=0, keepdims=True)
    shift = jnp.max(shift_ref[...])
    y_all = jnp.concatenate([y, extra_rows(y_norm + line_up(sample) + shift)], axis=0)
    right = jnp.concatenate([y, y, y, y, jnp.ones((LANES, SAMPLES), BF16)], axis=0)
    x = x_ref[...]
    total = jnp.zeros((POINTS, 2 * LANES), F32)
    for chunk in range(8):
        cols = slice(chunk * 256, chunk * 256 + 256)
        weight = jnp.exp2(jnp.dot(x, y_all[:, cols], preferred_element_type=F32) * SCALE)
        total += lax.dot_general(
            weight.astype(BF16),
            right[:, cols],
            (((1,), (1,)), ((), ())),
            preferred_element_type=F32,
        )
    numer = total[:, :LANES].reshape(16, 4, 8, LANES)
    denom = total[:, LANES:].reshape(16, 4, 8, LANES)
    shape = (16, 8, LANES)
    lane, row = lanes_of(shape), rows_of(shape)
    first, second = numer[:, 0], jnp.where(lane == row, denom[:, 0], 0.0)
    for q in range(1, 4):
        first = jnp.where(lane // 32 == q, numer[:, q], first)
        second = jnp.where(lane == row + 8 * q, denom[:, q], second)
    second = jnp.sum(second, axis=1)
    for peer in range(16):
        parts_out[9 * peer : 9 * peer + 8, :] = first[peer]
        parts_out[9 * peer + 8 : 9 * peer + 9, :] = second[peer : peer + 1]


def finish(parts_ref, bary_out):
    numer, denom = parts_ref[:8, :], parts_ref[8:9, :]
    for peer in range(1, 16):
        numer = numer + parts_ref[9 * peer : 9 * peer + 8, :]
        denom = denom + parts_ref[9 * peer + 8 : 9 * peer + 9, :]
    stack = [numer] + [pltpu.roll(numer, LANES - 32 * q, 1) for q in range(1, 4)]
    bary_out[...] = turned(jnp.concatenate(stack, axis=0))[:32, :32] / denom[:, :32]


def exchange(value, axes, first):
    count = lax.axis_size(axes)
    order = [(first + k) % count for k in range(count)]
    return lax.all_to_all(value, axes, 0, 0, axis_index_groups=[order])


def call(body, outs, *args):
    vmem = pl.BlockSpec(memory_space=pltpu.VMEM)
    return pl.pallas_call(
        body,
        out_shape=[jax.ShapeDtypeStruct(shape, dtype) for shape, dtype in outs],
        in_specs=[vmem] * len(args),
        out_specs=[vmem] * len(outs),
        compiler_params=pltpu.CompilerParams(vmem_limit_bytes=8 << 20),
    )(*args)


def on_device(points, samples, potential):
    (xs,) = call(prepare_points, [((16, 8, LANES), BF16)], points)
    xs = exchange(xs, "z", 10).reshape(LANES, LANES)
    (own,) = call(prepare_samples, [((40, 512), BF16)], samples, potential.reshape(1, 512))
    ys = lax.all_gather(own, ("x_hi", "core"))
    x, y, rows = call(
        row_pass,
        [((POINTS, DEPTH), BF16), ((DEPTH, SAMPLES), BF16), ((16, 4, LANES), F32)],
        xs, ys,
    )
    rows = exchange(rows, "z", 10)
    x, shift, cols, point = call(
        col_pass,
        [((POINTS, DEPTH), BF16), ((1, LANES), F32), ((32, 16, LANES), F32), ((1, 32), F32)],
        x, y, rows,
    )
    cols = exchange(cols, PLANE, 10)
    parts, sample = call(
        weigh, [((144, LANES), F32), ((4, LANES), F32)], x, y, shift, cols
    )
    parts = parts.reshape(16, 9, 1, LANES)
    parts = exchange(parts, "z", 10).reshape(144, LANES)
    (bary,) = call(finish, [((32, 32), F32)], parts)
    return point.reshape(32), sample.reshape(512), bary


def solution(mesh):
    split = Mesh(mesh.devices.reshape(SHAPE), AXES)
    cols = ("z", "x_hi", "core")
    return jax.shard_map(
        on_device,
        mesh=split,
        in_specs=(P(None, AXES), P(None, cols), P(cols)),
        out_specs=(P(AXES), P(cols), P(None, AXES)),
        check_vma=False,
    )
```

```python
import math

import jax
import jax.numpy as jnp
from jax import lax
from jax.experimental import pallas as pl
from jax.experimental.pallas import tpu as pltpu
from jax.sharding import Mesh, PartitionSpec as P

EPS = 0.25
SCALE = math.log2(math.e) / EPS
MARGIN = 18.0
AXES = ("x_lo", "y", "z", "x_hi", "core")
SHAPE = (2, 4, 16, 2, 2)
PLANE = ("x_lo", "y", "x_hi", "core")
POINTS = 512
SAMPLES = 2048
LOG_POINTS = math.log2(POINTS * 32)
LOG_SAMPLES = math.log2(SAMPLES * 16)
LANES = 128
DEPTH = 48
F32 = jnp.float32
BF16 = jnp.bfloat16


def lanes_of(shape):
    return lax.broadcasted_iota(jnp.int32, shape, len(shape) - 1)


def rows_of(shape):
    return lax.broadcasted_iota(jnp.int32, shape, len(shape) - 2)


def triple(value):
    high = value.astype(BF16).astype(F32)
    rest = value - high
    mid = rest.astype(BF16).astype(F32)
    return high, mid, rest - mid


def turned(block):
    rows, cols = block.shape
    if rows < LANES:
        block = jnp.concatenate([block, jnp.zeros((LANES - rows, cols), block.dtype)], axis=0)
    return jnp.transpose(block)


def product(left, right):
    return lax.dot_general(left, right, (((1,), (1,)), ((), ())), preferred_element_type=F32)


def combine(lse):
    top = jnp.max(lse, axis=0)
    return top + jnp.log2(jnp.sum(jnp.exp2(lse - top[None]), axis=0))


def line_up(block):
    return jnp.concatenate([block[k : k + 1] for k in range(block.shape[0])], axis=1)


def stack_up(lines):
    lane = rows_of((len(lines), LANES))
    block = jnp.broadcast_to(lines[0], lane.shape)
    for k, line in enumerate(lines[1:], 1):
        block = jnp.where(lane == k, line, block)
    return block


def extra_rows(value):
    row = rows_of((16, value.shape[1]))
    block = jnp.where((row >= 3) & (row < 9), 1.0, 0.0)
    for k, part in enumerate(triple(value)):
        block = jnp.where(row == k, part, block)
    return block.astype(BF16)


def prepare_points(points_ref, points_out):
    x = turned(points_ref[...].astype(F32))
    packed = x[:8]
    for q in range(1, 4):
        packed = packed + pltpu.roll(x[8 * q : 8 * q + 8], 32 * q, 1)
    points_out[...] = jnp.broadcast_to(packed.astype(BF16)[None], (16, 8, LANES))


def prepare_samples(samples_ref, potential_ref, samples_out):
    samples_out[:32, :] = samples_ref[...]
    pot = potential_ref[...]
    row = rows_of((8, 512))
    block = jnp.zeros((8, 512), F32)
    for k, part in enumerate(triple(pot)):
        block = jnp.where(row == k, part, block)
    samples_out[32:, :] = block.astype(BF16)


def row_pass(points_ref, samples_ref, x_out, y_out, lse_out):
    packed = points_ref[...].astype(F32)
    x = jnp.concatenate(
        [packed.reshape(16, 1, 8, LANES)]
        + [pltpu.roll(packed, LANES - 32 * q, 1).reshape(16, 1, 8, LANES) for q in range(1, 4)],
        axis=1,
    ).reshape(POINTS, LANES)
    lane = lanes_of(x.shape)
    x = jnp.where(lane < 32, x, 0.0)
    x_norm = -0.5 * jnp.sum(x * x, axis=1, keepdims=True)
    x = jnp.where((lane >= 32) & (lane < 35), 1.0, x)
    for k, part in enumerate(triple(x_norm)):
        x = jnp.where(lane == 35 + k, part, x)
    x = x[:, :DEPTH].astype(BF16)
    x_out[...] = x
    y = jnp.concatenate([samples_ref[k].astype(F32) for k in range(4)], axis=1)
    pot = jnp.sum(y[32:40], axis=0, keepdims=True)
    y = y[:32]
    y_norm = -0.5 * jnp.sum(y * y, axis=0, keepdims=True)
    shift = jnp.max(pot) - MARGIN
    y_out[:32, :] = y.astype(BF16)
    y_out[32:, :] = extra_rows(y_norm)
    y = jnp.concatenate([y.astype(BF16), extra_rows(y_norm + pot - shift)], axis=0)
    lines = []
    for tile in range(4):
        total = jnp.zeros((LANES, LANES), F32)
        left = x[tile * 128 : tile * 128 + 128]
        for chunk in range(8):
            right = y[:, chunk * 256 : chunk * 256 + 256]
            part = jnp.exp2(jnp.dot(left, right, preferred_element_type=F32) * SCALE)
            total += part[:, :LANES] + part[:, LANES:]
        line = jnp.transpose(total)
        line = jnp.sum(line, axis=0, keepdims=True)
        lines.append(jnp.log2(line) + SCALE * shift)
    lse_out[...] = jnp.broadcast_to(stack_up(lines)[None], (16, 4, LANES))


def col_pass(x_ref, y_ref, rows_ref, x_out, shift_out, lse_out, own_out):
    point = (LOG_SAMPLES - combine(rows_ref[...])) / SCALE
    z = lax.axis_index("z")
    z = sum(jnp.where(z == other, slot, 0) for slot, other in enumerate(Z_ORDER))
    line = jnp.sum(jnp.where(rows_of(point.shape) == z // 4, point, 0.0), axis=0, keepdims=True)
    line = pltpu.roll(jnp.broadcast_to(line, (8, LANES)), (4 - z % 4) * 32 % LANES, 1)
    own_out[...] = line[:1, :32]
    shift = jnp.max(point) - MARGIN
    shift_out[...] = jnp.full((1, LANES), shift, F32)
    parts = triple(point - shift)
    row = rows_of((DEPTH, LANES))
    blocks = []
    for tile in range(4):
        block = jnp.zeros((DEPTH, LANES), F32)
        for k, part in enumerate(parts):
            block = jnp.where(row == 38 + k, part[tile : tile + 1], block)
        blocks.append(jnp.transpose(block))
    x = (x_ref[...].astype(F32) + jnp.concatenate(blocks, axis=0)).astype(BF16)
    x_out[...] = x
    lines = []
    for chunk in range(8):
        right = y_ref[:, chunk * 256 : chunk * 256 + 256]
        total = jnp.zeros((8, 256), F32)
        for tile in range(4):
            left = x[tile * 128 : tile * 128 + 128]
            part = jnp.exp2(jnp.dot(left, right, preferred_element_type=F32) * SCALE)
            total += jnp.sum(part.reshape(16, 8, 256), axis=0)
        total = jnp.log2(jnp.sum(total, axis=0, keepdims=True)) + SCALE * shift
        lines += [total[:, :LANES], total[:, LANES:]]
    lse_out[...] = jnp.broadcast_to(stack_up(lines)[None], (32, 16, LANES))


def weigh(x_ref, y_ref, shift_ref, cols_ref, parts_out, sample_out):
    sample = (LOG_POINTS - combine(cols_ref[...])) / SCALE
    side = lax.axis_index("x_hi") * 2 + lax.axis_index("core")
    own = sample[:4]
    for k in range(1, 4):
        own = jnp.where(side == k, sample[4 * k : 4 * k + 4], own)
    sample_out[...] = own
    y = y_ref[:32, :]
    y_norm = jnp.sum(y_ref[32:, :].astype(F32)[:3], axis=0, keepdims=True)
    shift = jnp.max(shift_ref[...])
    y_all = jnp.concatenate([y, extra_rows(y_norm + line_up(sample) + shift)], axis=0)
    x = x_ref[...]
    right = jnp.concatenate([y, y, y, y, jnp.ones((128, SAMPLES), BF16)], axis=0)
    shape = (8, 8, LANES)
    lane, row = lanes_of(shape), rows_of(shape)
    for tile in range(2):
        weights = []
        for chunk in range(8):
            cols = slice(chunk * 256, chunk * 256 + 256)
            part = jnp.dot(x[tile * 256 : tile * 256 + 256], y_all[:, cols], preferred_element_type=F32)
            weights.append(jnp.exp2(part * SCALE).astype(BF16))
        total = product(jnp.concatenate(weights, axis=1), right)
        numer = total[:, :LANES].reshape(8, 4, 8, LANES)
        denom = total[:, LANES:]
        denom = denom.reshape(8, 4, 8, 128)
        first, second = numer[:, 0], jnp.where(lane[:, :, :128] == row[:, :, :128], denom[:, 0], 0.0)
        for q in range(1, 4):
            first = jnp.where(lane // 32 == q, numer[:, q], first)
            second = jnp.where(lane[:, :, :128] == row[:, :, :128] + 8 * q, denom[:, q], second)
        second = jnp.sum(second, axis=1)
        for part in range(8):
            peer = tile * 8 + part
            parts_out[9 * peer : 9 * peer + 8, :] = first[part]
            parts_out[9 * peer + 8 : 9 * peer + 9, :128] = second[part : part + 1]


def finish(parts_ref, bary_out):
    numer, denom = parts_ref[:8, :], parts_ref[8:9, :]
    for peer in range(1, 16):
        numer = numer + parts_ref[9 * peer : 9 * peer + 8, :]
        denom = denom + parts_ref[9 * peer + 8 : 9 * peer + 9, :]
    stack = [numer] + [pltpu.roll(numer, LANES - 32 * q, 1) for q in range(1, 4)]
    bary_out[...] = turned(jnp.concatenate(stack, axis=0))[:32, :32] / denom[:, :32]


Z_ORDER = (10, 11, 9, 12, 8, 13, 7, 14, 6, 15, 5, 0, 4, 1, 3, 2)
PLANE_ORDER = (10, 11, 12, 13, 14, 15, 16, 17, 18, 19, 20, 21, 22, 23, 24, 25, 26, 27, 28, 29, 30, 31, 0, 1, 2, 3, 4, 5, 6, 7, 8, 9)


def exchange(value, axes, order):
    return lax.all_to_all(value, axes, 0, 0, axis_index_groups=[list(order)])


def call(body, outs, *args):
    vmem = pl.BlockSpec(memory_space=pltpu.VMEM)
    return pl.pallas_call(
        body,
        out_shape=[jax.ShapeDtypeStruct(shape, dtype) for shape, dtype in outs],
        in_specs=[vmem] * len(args),
        out_specs=[vmem] * len(outs),
        compiler_params=pltpu.CompilerParams(vmem_limit_bytes=8 << 20),
    )(*args)


def on_device(points, samples, potential):
    (xs,) = call(prepare_points, [((16, 8, LANES), BF16)], points)
    xs = exchange(xs, "z", Z_ORDER).reshape(LANES, LANES)
    (own,) = call(prepare_samples, [((40, 512), BF16)], samples, potential.reshape(1, 512))
    ys = lax.all_gather(own, ("x_hi", "core"))
    x, y, rows = call(
        row_pass,
        [((POINTS, DEPTH), BF16), ((DEPTH, SAMPLES), BF16), ((16, 4, LANES), F32)],
        xs, ys,
    )
    rows = exchange(rows, "z", Z_ORDER)
    x, shift, cols, point = call(
        col_pass,
        [((POINTS, DEPTH), BF16), ((1, LANES), F32), ((32, 16, LANES), F32), ((1, 32), F32)],
        x, y, rows,
    )
    cols = exchange(cols, PLANE, PLANE_ORDER)
    parts, sample = call(
        weigh, [((144, LANES), F32), ((4, LANES), F32)], x, y, shift, cols
    )
    parts = parts.reshape(16, 9, 1, LANES)
    parts = exchange(parts, "z", Z_ORDER).reshape(144, LANES)
    (bary,) = call(finish, [((32, 32), F32)], parts)
    return point.reshape(32), sample.reshape(512), bary


def solution(mesh):
    split = Mesh(mesh.devices.reshape(SHAPE), AXES)
    cols = ("z", "x_hi", "core")
    return jax.shard_map(
        on_device,
        mesh=split,
        in_specs=(P(None, AXES), P(None, cols), P(cols)),
        out_specs=(P(AXES), P(cols), P(None, AXES)),
        check_vma=False,
    )
```

```python
import math

import jax
import jax.numpy as jnp
from jax import lax
from jax.experimental import pallas as pl
from jax.experimental.pallas import tpu as pltpu
from jax.sharding import Mesh, PartitionSpec as P

EPS = 0.25
SCALE = math.log2(math.e) / EPS
MARGIN = 18.0
AXES = ("x_lo", "y", "z", "x_hi", "core")
SHAPE = (2, 4, 16, 2, 2)
PLANE = ("x_lo", "y", "x_hi", "core")
POINTS = 512
SAMPLES = 2048
LOG_POINTS = math.log2(POINTS * 32)
LOG_SAMPLES = math.log2(SAMPLES * 16)
LANES = 128
DEPTH = 48
F32 = jnp.float32
BF16 = jnp.bfloat16


def lanes_of(shape):
    return lax.broadcasted_iota(jnp.int32, shape, len(shape) - 1)


def rows_of(shape):
    return lax.broadcasted_iota(jnp.int32, shape, len(shape) - 2)


def triple(value):
    high = value.astype(BF16).astype(F32)
    rest = value - high
    mid = rest.astype(BF16).astype(F32)
    return high, mid, rest - mid


def turned(block):
    rows, cols = block.shape
    if rows < LANES:
        block = jnp.concatenate([block, jnp.zeros((LANES - rows, cols), block.dtype)], axis=0)
    return jnp.transpose(block)


def product(left, right):
    return lax.dot_general(left, right, (((1,), (1,)), ((), ())), preferred_element_type=F32)


def combine(lse):
    top = jnp.max(lse, axis=0)
    return top + jnp.log2(jnp.sum(jnp.exp2(lse - top[None]), axis=0))


def line_up(block):
    return jnp.concatenate([block[k : k + 1] for k in range(block.shape[0])], axis=1)


def stack_up(lines):
    lane = rows_of((len(lines), LANES))
    block = jnp.broadcast_to(lines[0], lane.shape)
    for k, line in enumerate(lines[1:], 1):
        block = jnp.where(lane == k, line, block)
    return block


def extra_rows(value):
    row = rows_of((16, value.shape[1]))
    block = jnp.where((row >= 3) & (row < 9), 1.0, 0.0)
    for k, part in enumerate(triple(value)):
        block = jnp.where(row == k, part, block)
    return block.astype(BF16)


def prepare_points(points_ref, points_out):
    x = turned(points_ref[...].astype(F32))
    packed = x[:8]
    for q in range(1, 4):
        packed = packed + pltpu.roll(x[8 * q : 8 * q + 8], 32 * q, 1)
    points_out[...] = jnp.broadcast_to(packed.astype(BF16)[None], (16, 8, LANES))


def prepare_samples(samples_ref, potential_ref, samples_out):
    samples_out[:32, :] = samples_ref[...]
    pot = potential_ref[...]
    row = rows_of((8, 512))
    block = jnp.zeros((8, 512), F32)
    for k, part in enumerate(triple(pot)):
        block = jnp.where(row == k, part, block)
    samples_out[32:, :] = block.astype(BF16)


def row_pass(points_ref, samples_ref, x_out, y_out, lse_out):
    packed = points_ref[...].astype(F32)
    x = jnp.concatenate(
        [packed.reshape(16, 1, 8, LANES)]
        + [pltpu.roll(packed, LANES - 32 * q, 1).reshape(16, 1, 8, LANES) for q in range(1, 4)],
        axis=1,
    ).reshape(POINTS, LANES)
    lane = lanes_of(x.shape)
    x = jnp.where(lane < 32, x, 0.0)
    x_norm = -0.5 * jnp.sum(x * x, axis=1, keepdims=True)
    x = jnp.where((lane >= 32) & (lane < 35), 1.0, x)
    for k, part in enumerate(triple(x_norm)):
        x = jnp.where(lane == 35 + k, part, x)
    x = x[:, :DEPTH].astype(BF16)
    x_out[...] = x
    y = jnp.concatenate([samples_ref[k].astype(F32) for k in range(4)], axis=1)
    pot = jnp.sum(y[32:40], axis=0, keepdims=True)
    y = y[:32]
    y_norm = -0.5 * jnp.sum(y * y, axis=0, keepdims=True)
    shift = jnp.max(pot) - MARGIN
    y_out[:32, :] = y.astype(BF16)
    y_out[32:, :] = extra_rows(y_norm)
    y = jnp.concatenate([y.astype(BF16), extra_rows(y_norm + pot - shift)], axis=0)
    lines = []
    for tile in range(4):
        total = jnp.zeros((LANES, LANES), F32)
        left = x[tile * 128 : tile * 128 + 128]
        for chunk in range(8):
            right = y[:, chunk * 256 : chunk * 256 + 256]
            part = jnp.exp2(jnp.dot(left, right, preferred_element_type=F32) * SCALE)
            total += part[:, :LANES] + part[:, LANES:]
        line = jnp.transpose(total)
        line = jnp.sum(line, axis=0, keepdims=True)
        lines.append(jnp.log2(line) + SCALE * shift)
    lse_out[...] = jnp.broadcast_to(stack_up(lines)[None], (16, 4, LANES))


def col_pass(x_ref, y_ref, rows_ref, x_out, shift_out, lse_out, own_out):
    point = (LOG_SAMPLES - combine(rows_ref[...])) / SCALE
    z = lax.axis_index("z")
    z = sum(jnp.where(z == other, slot, 0) for slot, other in enumerate(Z_ORDER))
    line = jnp.sum(jnp.where(rows_of(point.shape) == z // 4, point, 0.0), axis=0, keepdims=True)
    line = pltpu.roll(jnp.broadcast_to(line, (8, LANES)), (4 - z % 4) * 32 % LANES, 1)
    own_out[...] = line[:1, :32]
    shift = jnp.max(point) - MARGIN
    shift_out[...] = jnp.full((1, LANES), shift, F32)
    parts = triple(point - shift)
    row = rows_of((DEPTH, LANES))
    blocks = []
    for tile in range(4):
        block = jnp.zeros((DEPTH, LANES), F32)
        for k, part in enumerate(parts):
            block = jnp.where(row == 38 + k, part[tile : tile + 1], block)
        blocks.append(jnp.transpose(block))
    x = (x_ref[...].astype(F32) + jnp.concatenate(blocks, axis=0)).astype(BF16)
    x_out[...] = x
    lines = []
    for chunk in range(8):
        right = y_ref[:, chunk * 256 : chunk * 256 + 256]
        total = jnp.zeros((8, 256), F32)
        for tile in range(4):
            left = x[tile * 128 : tile * 128 + 128]
            part = jnp.exp2(jnp.dot(left, right, preferred_element_type=F32) * SCALE)
            total += jnp.sum(part.reshape(16, 8, 256), axis=0)
        total = jnp.log2(jnp.sum(total, axis=0, keepdims=True)) + SCALE * shift
        lines += [total[:, :LANES], total[:, LANES:]]
    lse_out[...] = jnp.broadcast_to(stack_up(lines)[None], (32, 16, LANES))


def weigh(x_ref, y_ref, shift_ref, cols_ref, parts_out, sample_out):
    sample = (LOG_POINTS - combine(cols_ref[...])) / SCALE
    side = lax.axis_index("x_hi") * 2 + lax.axis_index("core")
    own = sample[:4]
    for k in range(1, 4):
        own = jnp.where(side == k, sample[4 * k : 4 * k + 4], own)
    sample_out[...] = own
    y = y_ref[:32, :]
    y_norm = jnp.sum(y_ref[32:, :].astype(F32)[:3], axis=0, keepdims=True)
    shift = jnp.max(shift_ref[...])
    y_all = jnp.concatenate([y, extra_rows(y_norm + line_up(sample) + shift)], axis=0)
    x = x_ref[...]
    right = jnp.concatenate([y, y, y, y, jnp.ones((128, SAMPLES), BF16)], axis=0)
    shape = (8, 8, LANES)
    lane, row = lanes_of(shape), rows_of(shape)
    for tile in range(2):
        weights = []
        for chunk in range(8):
            cols = slice(chunk * 256, chunk * 256 + 256)
            part = jnp.dot(x[tile * 256 : tile * 256 + 256], y_all[:, cols], preferred_element_type=F32)
            weights.append(jnp.exp2(part * SCALE).astype(BF16))
        total = product(jnp.concatenate(weights, axis=1), right)
        numer = total[:, :LANES].reshape(8, 4, 8, LANES)
        denom = total[:, LANES:]
        denom = denom.reshape(8, 4, 8, 128)
        first, second = numer[:, 0], jnp.where(lane[:, :, :128] == row[:, :, :128], denom[:, 0], 0.0)
        for q in range(1, 4):
            first = jnp.where(lane // 32 == q, numer[:, q], first)
            second = jnp.where(lane[:, :, :128] == row[:, :, :128] + 8 * q, denom[:, q], second)
        second = jnp.sum(second, axis=1)
        for part in range(8):
            peer = Z_PARTS.index(Z_ORDER[tile * 8 + part])
            parts_out[9 * peer : 9 * peer + 8, :] = first[part]
            parts_out[9 * peer + 8 : 9 * peer + 9, :128] = second[part : part + 1]


def finish(parts_ref, bary_out):
    numer, denom = parts_ref[:8, :], parts_ref[8:9, :]
    for peer in range(1, 16):
        numer = numer + parts_ref[9 * peer : 9 * peer + 8, :]
        denom = denom + parts_ref[9 * peer + 8 : 9 * peer + 9, :]
    stack = [numer] + [pltpu.roll(numer, LANES - 32 * q, 1) for q in range(1, 4)]
    bary_out[...] = turned(jnp.concatenate(stack, axis=0))[:32, :32] / denom[:, :32]


Z_ORDER = (11, 12, 10, 13, 9, 14, 8, 15, 7, 0, 6, 1, 5, 2, 4, 3)
Z_ROWS = (9, 10, 8, 11, 7, 12, 6, 13, 5, 14, 4, 15, 3, 0, 2, 1)
Z_PARTS = (8, 9, 7, 10, 6, 11, 5, 12, 4, 13, 3, 14, 2, 15, 1, 0)
PLANE_ORDER = (10, 11, 12, 13, 14, 15, 16, 17, 18, 19, 20, 21, 22, 23, 24, 25, 26, 27, 28, 29, 30, 31, 0, 1, 2, 3, 4, 5, 6, 7, 8, 9)


def exchange(value, axes, order):
    return lax.all_to_all(value, axes, 0, 0, axis_index_groups=[list(order)])


def call(body, outs, *args):
    vmem = pl.BlockSpec(memory_space=pltpu.VMEM)
    return pl.pallas_call(
        body,
        out_shape=[jax.ShapeDtypeStruct(shape, dtype) for shape, dtype in outs],
        in_specs=[vmem] * len(args),
        out_specs=[vmem] * len(outs),
        compiler_params=pltpu.CompilerParams(vmem_limit_bytes=8 << 20),
    )(*args)


def on_device(points, samples, potential):
    (xs,) = call(prepare_points, [((16, 8, LANES), BF16)], points)
    xs = exchange(xs, "z", Z_ORDER).reshape(LANES, LANES)
    (own,) = call(prepare_samples, [((40, 512), BF16)], samples, potential.reshape(1, 512))
    ys = lax.all_gather(own, ("x_hi", "core"))
    x, y, rows = call(
        row_pass,
        [((POINTS, DEPTH), BF16), ((DEPTH, SAMPLES), BF16), ((16, 4, LANES), F32)],
        xs, ys,
    )
    rows = exchange(rows, "z", Z_ROWS)
    x, shift, cols, point = call(
        col_pass,
        [((POINTS, DEPTH), BF16), ((1, LANES), F32), ((32, 16, LANES), F32), ((1, 32), F32)],
        x, y, rows,
    )
    cols = exchange(cols, PLANE, PLANE_ORDER)
    parts, sample = call(
        weigh, [((144, LANES), F32), ((4, LANES), F32)], x, y, shift, cols
    )
    parts = parts.reshape(16, 9, 1, LANES)
    parts = exchange(parts, "z", Z_PARTS).reshape(144, LANES)
    (bary,) = call(finish, [((32, 32), F32)], parts)
    return point.reshape(32), sample.reshape(512), bary


def solution(mesh):
    split = Mesh(mesh.devices.reshape(SHAPE), AXES)
    cols = ("z", "x_hi", "core")
    return jax.shard_map(
        on_device,
        mesh=split,
        in_specs=(P(None, AXES), P(None, cols), P(cols)),
        out_specs=(P(AXES), P(cols), P(None, AXES)),
        check_vma=False,
    )
```

```python
import math

import jax
import jax.numpy as jnp
from jax import lax
from jax.experimental import pallas as pl
from jax.experimental.pallas import tpu as pltpu
from jax.sharding import Mesh, PartitionSpec as P

EPS = 0.25
SCALE = math.log2(math.e) / EPS
MARGIN = 18.0
AXES = ("x_lo", "y", "z", "x_hi", "core")
SHAPE = (2, 4, 16, 2, 2)
PLANE = ("x_lo", "y", "x_hi", "core")
POINTS = 512
SAMPLES = 2048
LOG_POINTS = math.log2(POINTS * 32)
LOG_SAMPLES = math.log2(SAMPLES * 16)
LANES = 128
DEPTH = 48
F32 = jnp.float32
BF16 = jnp.bfloat16


def lanes_of(shape):
    return lax.broadcasted_iota(jnp.int32, shape, len(shape) - 1)


def rows_of(shape):
    return lax.broadcasted_iota(jnp.int32, shape, len(shape) - 2)


def triple(value):
    high = value.astype(BF16).astype(F32)
    rest = value - high
    mid = rest.astype(BF16).astype(F32)
    return high, mid, rest - mid


def turned(block):
    rows, cols = block.shape
    if rows < LANES:
        block = jnp.concatenate([block, jnp.zeros((LANES - rows, cols), block.dtype)], axis=0)
    return jnp.transpose(block)


def product(left, right):
    return lax.dot_general(left, right, (((1,), (1,)), ((), ())), preferred_element_type=F32)


def combine(lse):
    top = jnp.max(lse, axis=0)
    return top + jnp.log2(jnp.sum(jnp.exp2(lse - top[None]), axis=0))


def line_up(block):
    return jnp.concatenate([block[k : k + 1] for k in range(block.shape[0])], axis=1)


def stack_up(lines):
    lane = rows_of((len(lines), LANES))
    block = jnp.broadcast_to(lines[0], lane.shape)
    for k, line in enumerate(lines[1:], 1):
        block = jnp.where(lane == k, line, block)
    return block


def extra_rows(value):
    row = rows_of((16, value.shape[1]))
    block = jnp.where((row >= 3) & (row < 9), 1.0, 0.0)
    for k, part in enumerate(triple(value)):
        block = jnp.where(row == k, part, block)
    return block.astype(BF16)


def prepare_points(points_ref, points_out):
    x = turned(points_ref[...].astype(F32))
    packed = x[:8]
    for q in range(1, 4):
        packed = packed + pltpu.roll(x[8 * q : 8 * q + 8], 32 * q, 1)
    points_out[...] = jnp.broadcast_to(packed.astype(BF16)[None], (16, 8, LANES))


def prepare_samples(samples_ref, potential_ref, samples_out):
    samples_out[:32, :] = samples_ref[...]
    pot = potential_ref[...]
    row = rows_of((8, 512))
    block = jnp.zeros((8, 512), F32)
    for k, part in enumerate(triple(pot)):
        block = jnp.where(row == k, part, block)
    samples_out[32:, :] = block.astype(BF16)


def row_pass(points_ref, samples_ref, x_out, y_out, lse_out):
    packed = points_ref[...].astype(F32)
    x = jnp.concatenate(
        [packed.reshape(16, 1, 8, LANES)]
        + [pltpu.roll(packed, LANES - 32 * q, 1).reshape(16, 1, 8, LANES) for q in range(1, 4)],
        axis=1,
    ).reshape(POINTS, LANES)
    lane = lanes_of(x.shape)
    x = jnp.where(lane < 32, x, 0.0)
    x_norm = -0.5 * jnp.sum(x * x, axis=1, keepdims=True)
    x = jnp.where((lane >= 32) & (lane < 35), 1.0, x)
    for k, part in enumerate(triple(x_norm)):
        x = jnp.where(lane == 35 + k, part, x)
    x = x[:, :DEPTH].astype(BF16)
    x_out[...] = x
    y = jnp.concatenate([samples_ref[k].astype(F32) for k in range(4)], axis=1)
    pot = jnp.sum(y[32:40], axis=0, keepdims=True)
    y = y[:32]
    y_norm = -0.5 * jnp.sum(y * y, axis=0, keepdims=True)
    shift = jnp.max(pot) - MARGIN
    y_out[:32, :] = y.astype(BF16)
    y_out[32:, :] = extra_rows(y_norm)
    y = jnp.concatenate([y.astype(BF16), extra_rows(y_norm + pot - shift)], axis=0)
    lines = []
    for tile in range(4):
        total = jnp.zeros((LANES, LANES), F32)
        left = x[tile * 128 : tile * 128 + 128]
        for chunk in range(8):
            right = y[:, chunk * 256 : chunk * 256 + 256]
            part = jnp.exp2(jnp.dot(left, right, preferred_element_type=F32) * SCALE)
            total += part[:, :LANES] + part[:, LANES:]
        line = jnp.transpose(total)
        line = jnp.sum(line, axis=0, keepdims=True)
        lines.append(jnp.log2(line) + SCALE * shift)
    lse_out[...] = jnp.broadcast_to(stack_up(lines)[None], (16, 4, LANES))


def col_pass(x_ref, y_ref, rows_ref, x_out, shift_out, sums_out, own_out):
    point = (LOG_SAMPLES - combine(rows_ref[...])) / SCALE
    z = lax.axis_index("z")
    z = sum(jnp.where(z == other, slot, 0) for slot, other in enumerate(Z_ORDER))
    line = jnp.sum(jnp.where(rows_of(point.shape) == z // 4, point, 0.0), axis=0, keepdims=True)
    line = pltpu.roll(jnp.broadcast_to(line, (8, LANES)), (4 - z % 4) * 32 % LANES, 1)
    own_out[...] = line[:1, :32]
    shift = jnp.max(point) - MARGIN
    shift_out[...] = jnp.full((1, LANES), shift, F32)
    parts = triple(point - shift)
    row = rows_of((DEPTH, LANES))
    blocks = []
    for tile in range(4):
        block = jnp.zeros((DEPTH, LANES), F32)
        for k, part in enumerate(parts):
            block = jnp.where(row == 38 + k, part[tile : tile + 1], block)
        blocks.append(jnp.transpose(block))
    x = (x_ref[...].astype(F32) + jnp.concatenate(blocks, axis=0)).astype(BF16)
    x_out[...] = x
    lines = []
    for chunk in range(8):
        right = y_ref[:, chunk * 256 : chunk * 256 + 256]
        total = jnp.zeros((8, 256), F32)
        for tile in range(4):
            left = x[tile * 128 : tile * 128 + 128]
            part = jnp.exp2(jnp.dot(left, right, preferred_element_type=F32) * SCALE)
            total += jnp.sum(part.reshape(16, 8, 256), axis=0)
        total = jnp.sum(total, axis=0, keepdims=True)
        lines += [total[:, :LANES], total[:, LANES:]]
    lane = lanes_of((8, LANES))
    block = jnp.zeros((8, LANES), F32)
    for k, part in enumerate(triple(jnp.full((1, LANES), shift, F32))):
        block = jnp.where(lane == k, part, block)
    block = jnp.concatenate([stack_up(lines), block], axis=0).astype(BF16)
    sums_out[...] = jnp.broadcast_to(block[None], (32, 24, LANES))


def weigh(x_ref, y_ref, shift_ref, cols_ref, parts_out, sample_out):
    cols = cols_ref[...].astype(F32)
    moved = jnp.sum(cols[:, 16:], axis=(1, 2), keepdims=True) / 8
    most = jnp.max(moved)
    total = jnp.sum(cols[:, :16] * jnp.exp2((moved - most) * SCALE), axis=0)
    sample = (LOG_POINTS - jnp.log2(total)) / SCALE - most
    side = lax.axis_index("x_hi") * 2 + lax.axis_index("core")
    own = sample[:4]
    for k in range(1, 4):
        own = jnp.where(side == k, sample[4 * k : 4 * k + 4], own)
    sample_out[...] = own
    y = y_ref[:32, :]
    y_norm = jnp.sum(y_ref[32:, :].astype(F32)[:3], axis=0, keepdims=True)
    shift = jnp.max(shift_ref[...])
    y_all = jnp.concatenate([y, extra_rows(y_norm + line_up(sample) + shift)], axis=0)
    x = x_ref[...]
    right = jnp.concatenate([y, y, y, y, jnp.ones((128, SAMPLES), BF16)], axis=0)
    shape = (8, 8, LANES)
    lane, row = lanes_of(shape), rows_of(shape)
    for tile in range(2):
        weights = []
        for chunk in range(8):
            cols = slice(chunk * 256, chunk * 256 + 256)
            part = jnp.dot(x[tile * 256 : tile * 256 + 256], y_all[:, cols], preferred_element_type=F32)
            weights.append(jnp.exp2(part * SCALE).astype(BF16))
        total = product(jnp.concatenate(weights, axis=1), right)
        numer = total[:, :LANES].reshape(8, 4, 8, LANES)
        denom = total[:, LANES:]
        denom = denom.reshape(8, 4, 8, 128)
        first, second = numer[:, 0], jnp.where(lane[:, :, :128] == row[:, :, :128], denom[:, 0], 0.0)
        for q in range(1, 4):
            first = jnp.where(lane // 32 == q, numer[:, q], first)
            second = jnp.where(lane[:, :, :128] == row[:, :, :128] + 8 * q, denom[:, q], second)
        second = jnp.sum(second, axis=1)
        for part in range(8):
            peer = Z_PARTS.index(Z_ORDER[tile * 8 + part])
            parts_out[9 * peer : 9 * peer + 8, :] = first[part]
            parts_out[9 * peer + 8 : 9 * peer + 9, :128] = second[part : part + 1]


def finish(parts_ref, bary_out):
    numer, denom = parts_ref[:8, :], parts_ref[8:9, :]
    for peer in range(1, 16):
        numer = numer + parts_ref[9 * peer : 9 * peer + 8, :]
        denom = denom + parts_ref[9 * peer + 8 : 9 * peer + 9, :]
    stack = [numer] + [pltpu.roll(numer, LANES - 32 * q, 1) for q in range(1, 4)]
    bary_out[...] = turned(jnp.concatenate(stack, axis=0))[:32, :32] / denom[:, :32]


Z_ORDER = (11, 12, 10, 13, 9, 14, 8, 15, 7, 0, 6, 1, 5, 2, 4, 3)
Z_ROWS = (9, 10, 8, 11, 7, 12, 6, 13, 5, 14, 4, 15, 3, 0, 2, 1)
Z_PARTS = (8, 9, 7, 10, 6, 11, 5, 12, 4, 13, 3, 14, 2, 15, 1, 0)
PLANE_ORDER = (10, 11, 12, 13, 14, 15, 16, 17, 18, 19, 20, 21, 22, 23, 24, 25, 26, 27, 28, 29, 30, 31, 0, 1, 2, 3, 4, 5, 6, 7, 8, 9)


def exchange(value, axes, order):
    return lax.all_to_all(value, axes, 0, 0, axis_index_groups=[list(order)])


def call(body, outs, *args):
    vmem = pl.BlockSpec(memory_space=pltpu.VMEM)
    return pl.pallas_call(
        body,
        out_shape=[jax.ShapeDtypeStruct(shape, dtype) for shape, dtype in outs],
        in_specs=[vmem] * len(args),
        out_specs=[vmem] * len(outs),
        compiler_params=pltpu.CompilerParams(vmem_limit_bytes=8 << 20),
    )(*args)


def on_device(points, samples, potential):
    (xs,) = call(prepare_points, [((16, 8, LANES), BF16)], points)
    xs = exchange(xs, "z", Z_ORDER).reshape(LANES, LANES)
    (own,) = call(prepare_samples, [((40, 512), BF16)], samples, potential.reshape(1, 512))
    ys = lax.all_gather(own, ("x_hi", "core"))
    x, y, rows = call(
        row_pass,
        [((POINTS, DEPTH), BF16), ((DEPTH, SAMPLES), BF16), ((16, 4, LANES), F32)],
        xs, ys,
    )
    rows = exchange(rows, "z", Z_ROWS)
    x, shift, cols, point = call(
        col_pass,
        [((POINTS, DEPTH), BF16), ((1, LANES), F32), ((32, 24, LANES), BF16), ((1, 32), F32)],
        x, y, rows,
    )
    cols = exchange(cols, PLANE, PLANE_ORDER)
    parts, sample = call(
        weigh, [((144, LANES), F32), ((4, LANES), F32)], x, y, shift, cols
    )
    parts = parts.reshape(16, 9, 1, LANES)
    parts = exchange(parts, "z", Z_PARTS).reshape(144, LANES)
    (bary,) = call(finish, [((32, 32), F32)], parts)
    return point.reshape(32), sample.reshape(512), bary


def solution(mesh):
    split = Mesh(mesh.devices.reshape(SHAPE), AXES)
    cols = ("z", "x_hi", "core")
    return jax.shard_map(
        on_device,
        mesh=split,
        in_specs=(P(None, AXES), P(None, cols), P(cols)),
        out_specs=(P(AXES), P(cols), P(None, AXES)),
        check_vma=False,
    )
```

```python
import math

import jax
import jax.numpy as jnp
from jax import lax
from jax.experimental import pallas as pl
from jax.experimental.pallas import tpu as pltpu
from jax.sharding import Mesh, PartitionSpec as P

EPS = 0.25
SCALE = math.log2(math.e) / EPS
MARGIN = 18.0
AXES = ("x_lo", "y", "z", "x_hi", "core")
SHAPE = (2, 4, 16, 2, 2)
PLANE = ("x_lo", "y", "x_hi", "core")
POINTS = 512
SAMPLES = 2048
LOG_POINTS = math.log2(POINTS * 32)
LOG_SAMPLES = math.log2(SAMPLES * 16)
LANES = 128
DEPTH = 48
F32 = jnp.float32
BF16 = jnp.bfloat16


def lanes_of(shape):
    return lax.broadcasted_iota(jnp.int32, shape, len(shape) - 1)


def rows_of(shape):
    return lax.broadcasted_iota(jnp.int32, shape, len(shape) - 2)


def triple(value):
    high = value.astype(BF16).astype(F32)
    rest = value - high
    mid = rest.astype(BF16).astype(F32)
    return high, mid, rest - mid


def turned(block):
    rows, cols = block.shape
    if rows < LANES:
        block = jnp.concatenate([block, jnp.zeros((LANES - rows, cols), block.dtype)], axis=0)
    return jnp.transpose(block)


def product(left, right):
    return lax.dot_general(left, right, (((1,), (1,)), ((), ())), preferred_element_type=F32)


def combine(lse):
    top = jnp.max(lse, axis=0)
    return top + jnp.log2(jnp.sum(jnp.exp2(lse - top[None]), axis=0))


def line_up(block):
    return jnp.concatenate([block[k : k + 1] for k in range(block.shape[0])], axis=1)


def stack_up(lines):
    lane = rows_of((len(lines), LANES))
    block = jnp.broadcast_to(lines[0], lane.shape)
    for k, line in enumerate(lines[1:], 1):
        block = jnp.where(lane == k, line, block)
    return block


def extra_rows(value):
    row = rows_of((16, value.shape[1]))
    block = jnp.where((row >= 3) & (row < 9), 1.0, 0.0)
    for k, part in enumerate(triple(value)):
        block = jnp.where(row == k, part, block)
    return block.astype(BF16)


def prepare_points(points_ref, points_out):
    x = turned(points_ref[...].astype(F32))
    packed = x[:8]
    for q in range(1, 4):
        packed = packed + pltpu.roll(x[8 * q : 8 * q + 8], 32 * q, 1)
    points_out[...] = jnp.broadcast_to(packed.astype(BF16)[None], (16, 8, LANES))


def prepare_samples(samples_ref, potential_ref, samples_out):
    samples_out[:32, :] = samples_ref[...]
    pot = potential_ref[...]
    row = rows_of((8, 512))
    block = jnp.zeros((8, 512), F32)
    for k, part in enumerate(triple(pot)):
        block = jnp.where(row == k, part, block)
    samples_out[32:, :] = block.astype(BF16)


def row_pass(points_ref, samples_ref, x_out, y_out, lse_out):
    packed = points_ref[...].astype(F32)
    x = jnp.concatenate(
        [packed.reshape(16, 1, 8, LANES)]
        + [pltpu.roll(packed, LANES - 32 * q, 1).reshape(16, 1, 8, LANES) for q in range(1, 4)],
        axis=1,
    ).reshape(POINTS, LANES)
    lane = lanes_of(x.shape)
    x = jnp.where(lane < 32, x, 0.0)
    x_norm = -0.5 * jnp.sum(x * x, axis=1, keepdims=True)
    x = jnp.where((lane >= 32) & (lane < 35), 1.0, x)
    for k, part in enumerate(triple(x_norm)):
        x = jnp.where(lane == 35 + k, part, x)
    x = x[:, :DEPTH].astype(BF16)
    x_out[...] = x
    y = jnp.concatenate([samples_ref[k].astype(F32) for k in range(4)], axis=1)
    pot = jnp.sum(y[32:40], axis=0, keepdims=True)
    y = y[:32]
    y_norm = -0.5 * jnp.sum(y * y, axis=0, keepdims=True)
    shift = jnp.max(pot) - MARGIN
    y_out[:32, :] = y.astype(BF16)
    y_out[32:, :] = extra_rows(y_norm)
    y = jnp.concatenate([y.astype(BF16), extra_rows(y_norm + pot - shift)], axis=0)
    lines = []
    for tile in range(4):
        total = jnp.zeros((LANES, LANES), F32)
        left = x[tile * 128 : tile * 128 + 128]
        for chunk in range(8):
            right = y[:, chunk * 256 : chunk * 256 + 256]
            part = jnp.exp2(jnp.dot(left, right, preferred_element_type=F32) * SCALE)
            total += part[:, :LANES] + part[:, LANES:]
        line = jnp.transpose(total)
        line = jnp.sum(line, axis=0, keepdims=True)
        lines.append(jnp.log2(line) + SCALE * shift)
    lse_out[...] = jnp.broadcast_to(stack_up(lines)[None], (16, 4, LANES))


def col_pass(x_ref, y_ref, rows_ref, x_out, shift_out, sums_out, own_out):
    point = (LOG_SAMPLES - combine(rows_ref[...])) / SCALE
    z = lax.axis_index("z")
    z = sum(jnp.where(z == other, slot, 0) for slot, other in enumerate(Z_ORDER))
    line = jnp.sum(jnp.where(rows_of(point.shape) == z // 4, point, 0.0), axis=0, keepdims=True)
    line = pltpu.roll(jnp.broadcast_to(line, (8, LANES)), (4 - z % 4) * 32 % LANES, 1)
    own_out[...] = line[:1, :32]
    shift = jnp.max(point) - MARGIN
    shift_out[...] = jnp.full((1, LANES), shift, F32)
    parts = triple(point - shift)
    row = rows_of((DEPTH, LANES))
    blocks = []
    for tile in range(4):
        block = jnp.zeros((DEPTH, LANES), F32)
        for k, part in enumerate(parts):
            block = jnp.where(row == 38 + k, part[tile : tile + 1], block)
        blocks.append(jnp.transpose(block))
    x = (x_ref[...].astype(F32) + jnp.concatenate(blocks, axis=0)).astype(BF16)
    x_out[...] = x
    lines = []
    for chunk in range(8):
        right = y_ref[:, chunk * 256 : chunk * 256 + 256]
        total = jnp.zeros((8, 256), F32)
        for tile in range(4):
            left = x[tile * 128 : tile * 128 + 128]
            part = jnp.exp2(jnp.dot(left, right, preferred_element_type=F32) * SCALE)
            total += jnp.sum(part.reshape(16, 8, 256), axis=0)
        total = jnp.sum(total, axis=0, keepdims=True)
        lines += [total[:, :LANES], total[:, LANES:]]
    lane = lanes_of((8, LANES))
    block = jnp.zeros((8, LANES), F32)
    for k, part in enumerate(triple(jnp.full((1, LANES), shift, F32))):
        block = jnp.where(lane == k, part, block)
    block = jnp.concatenate([stack_up(lines), block], axis=0).astype(BF16)
    sums_out[...] = jnp.broadcast_to(block[None], (32, 24, LANES))


def weigh(x_ref, y_ref, shift_ref, cols_ref, parts_out, sample_out):
    cols = cols_ref[...].astype(F32)
    moved = jnp.sum(cols[:, 16:], axis=(1, 2), keepdims=True) / 8
    most = jnp.max(moved)
    total = jnp.sum(cols[:, :16] * jnp.exp2((moved - most) * SCALE), axis=0)
    sample = (LOG_POINTS - jnp.log2(total)) / SCALE - most
    side = lax.axis_index("x_hi") * 2 + lax.axis_index("core")
    own = sample[:4]
    for k in range(1, 4):
        own = jnp.where(side == k, sample[4 * k : 4 * k + 4], own)
    sample_out[...] = own
    y = y_ref[:32, :]
    y_norm = jnp.sum(y_ref[32:, :].astype(F32)[:3], axis=0, keepdims=True)
    shift = jnp.max(shift_ref[...])
    y_all = jnp.concatenate([y, extra_rows(y_norm + line_up(sample) + shift)], axis=0)
    x = x_ref[...]
    right = jnp.concatenate([y, y, y, y, jnp.ones((128, SAMPLES), BF16)], axis=0)
    shape = (8, 8, LANES)
    lane, row = lanes_of(shape), rows_of(shape)
    for tile in range(2):
        weights = []
        for chunk in range(8):
            cols = slice(chunk * 256, chunk * 256 + 256)
            part = jnp.dot(x[tile * 256 : tile * 256 + 256], y_all[:, cols], preferred_element_type=F32)
            weights.append(jnp.exp2(part * SCALE).astype(BF16))
        total = product(jnp.concatenate(weights, axis=1), right)
        numer = total[:, :LANES].reshape(8, 4, 8, LANES)
        denom = total[:, LANES:]
        denom = denom.reshape(8, 4, 8, 128)
        first, second = numer[:, 0], jnp.where(lane[:, :, :128] == row[:, :, :128], denom[:, 0], 0.0)
        for q in range(1, 4):
            first = jnp.where(lane // 32 == q, numer[:, q], first)
            second = jnp.where(lane[:, :, :128] == row[:, :, :128] + 8 * q, denom[:, q], second)
        second = jnp.sum(second, axis=1)
        for part in range(8):
            peer = Z_PARTS.index(Z_ORDER[tile * 8 + part])
            parts_out[9 * peer : 9 * peer + 8, :] = first[part]
            parts_out[9 * peer + 8 : 9 * peer + 9, :128] = second[part : part + 1]


def finish(parts_ref, bary_out):
    numer, denom = parts_ref[:8, :], parts_ref[8:9, :]
    for peer in range(1, 16):
        numer = numer + parts_ref[9 * peer : 9 * peer + 8, :]
        denom = denom + parts_ref[9 * peer + 8 : 9 * peer + 9, :]
    stack = [numer] + [pltpu.roll(numer, LANES - 32 * q, 1) for q in range(1, 4)]
    bary_out[...] = turned(jnp.concatenate(stack, axis=0))[:32, :32] / denom[:, :32]


Z_ORDER = (12, 13, 11, 14, 10, 15, 9, 0, 8, 1, 7, 2, 6, 3, 5, 4)
Z_ROWS = (9, 10, 8, 11, 7, 12, 6, 13, 5, 14, 4, 15, 3, 0, 2, 1)
Z_PARTS = (8, 9, 7, 10, 6, 11, 5, 12, 4, 13, 3, 14, 2, 15, 1, 0)
PLANE_ORDER = (10, 11, 12, 13, 14, 15, 16, 17, 18, 19, 20, 21, 22, 23, 24, 25, 26, 27, 28, 29, 30, 31, 0, 1, 2, 3, 4, 5, 6, 7, 8, 9)


def exchange(value, axes, order):
    return lax.all_to_all(value, axes, 0, 0, axis_index_groups=[list(order)])


def call(body, outs, *args):
    vmem = pl.BlockSpec(memory_space=pltpu.VMEM)
    return pl.pallas_call(
        body,
        out_shape=[jax.ShapeDtypeStruct(shape, dtype) for shape, dtype in outs],
        in_specs=[vmem] * len(args),
        out_specs=[vmem] * len(outs),
        compiler_params=pltpu.CompilerParams(vmem_limit_bytes=8 << 20),
    )(*args)


def on_device(points, samples, potential):
    (xs,) = call(prepare_points, [((16, 8, LANES), BF16)], points)
    xs = exchange(xs, "z", Z_ORDER).reshape(LANES, LANES)
    (own,) = call(prepare_samples, [((40, 512), BF16)], samples, potential.reshape(1, 512))
    near = [[0, 1, 6, 7], [4, 5, 2, 3]]
    ys = lax.all_gather(own, ("x_lo", "x_hi", "core"), axis_index_groups=near)
    x, y, rows = call(
        row_pass,
        [((POINTS, DEPTH), BF16), ((DEPTH, SAMPLES), BF16), ((16, 4, LANES), F32)],
        xs, ys,
    )
    rows = exchange(rows, "z", Z_ROWS)
    x, shift, cols, point = call(
        col_pass,
        [((POINTS, DEPTH), BF16), ((1, LANES), F32), ((32, 24, LANES), BF16), ((1, 32), F32)],
        x, y, rows,
    )
    cols = exchange(cols, PLANE, PLANE_ORDER)
    parts, sample = call(
        weigh, [((144, LANES), F32), ((4, LANES), F32)], x, y, shift, cols
    )
    parts = parts.reshape(16, 9, 1, LANES)
    parts = exchange(parts, "z", Z_PARTS).reshape(144, LANES)
    (bary,) = call(finish, [((32, 32), F32)], parts)
    return point.reshape(32), sample.reshape(512), bary


def solution(mesh):
    split = Mesh(mesh.devices.reshape(SHAPE), AXES)
    cols = ("z", "x_hi", "core")
    return jax.shard_map(
        on_device,
        mesh=split,
        in_specs=(P(None, AXES), P(None, cols), P(cols)),
        out_specs=(P(AXES), P(cols), P(None, AXES)),
        check_vma=False,
    )
```

```python
import math

import jax
import jax.numpy as jnp
from jax import lax
from jax.experimental import pallas as pl
from jax.experimental.pallas import tpu as pltpu
from jax.sharding import Mesh, PartitionSpec as P

EPS = 0.25
SCALE = math.log2(math.e) / EPS
MARGIN = 18.0
AXES = ("x_lo", "y", "z", "x_hi", "core")
SHAPE = (2, 4, 16, 2, 2)
PLANE = ("x_lo", "y", "x_hi", "core")
POINTS = 512
SAMPLES = 2048
LOG_POINTS = math.log2(POINTS * 32)
LOG_SAMPLES = math.log2(SAMPLES * 16)
LANES = 128
DEPTH = 48
F32 = jnp.float32
BF16 = jnp.bfloat16


def lanes_of(shape):
    return lax.broadcasted_iota(jnp.int32, shape, len(shape) - 1)


def rows_of(shape):
    return lax.broadcasted_iota(jnp.int32, shape, len(shape) - 2)


def triple(value):
    high = value.astype(BF16).astype(F32)
    rest = value - high
    mid = rest.astype(BF16).astype(F32)
    return high, mid, rest - mid


def turned(block):
    rows, cols = block.shape
    if rows < LANES:
        block = jnp.concatenate([block, jnp.zeros((LANES - rows, cols), block.dtype)], axis=0)
    return jnp.transpose(block)


def product(left, right):
    return lax.dot_general(left, right, (((1,), (1,)), ((), ())), preferred_element_type=F32)


def combine(lse):
    top = jnp.max(lse, axis=0)
    return top + jnp.log2(jnp.sum(jnp.exp2(lse - top[None]), axis=0))


def line_up(block):
    return jnp.concatenate([block[k : k + 1] for k in range(block.shape[0])], axis=1)


def stack_up(lines):
    lane = rows_of((len(lines), LANES))
    block = jnp.broadcast_to(lines[0], lane.shape)
    for k, line in enumerate(lines[1:], 1):
        block = jnp.where(lane == k, line, block)
    return block


def extra_rows(value):
    row = rows_of((16, value.shape[1]))
    block = jnp.where((row >= 3) & (row < 9), 1.0, 0.0)
    for k, part in enumerate(triple(value)):
        block = jnp.where(row == k, part, block)
    return block.astype(BF16)


def prepare_points(points_ref, points_out):
    x = turned(points_ref[...].astype(F32))
    packed = x[:8]
    for q in range(1, 4):
        packed = packed + pltpu.roll(x[8 * q : 8 * q + 8], 32 * q, 1)
    points_out[...] = jnp.broadcast_to(packed.astype(BF16)[None], (16, 8, LANES))


def prepare_samples(samples_ref, potential_ref, samples_out):
    samples_out[:32, :] = samples_ref[...]
    pot = potential_ref[...]
    row = rows_of((8, 512))
    block = jnp.zeros((8, 512), F32)
    for k, part in enumerate(triple(pot)):
        block = jnp.where(row == k, part, block)
    samples_out[32:, :] = block.astype(BF16)


def row_pass(points_ref, samples_ref, x_out, y_out, lse_out):
    packed = points_ref[...].astype(F32)
    x = jnp.concatenate(
        [packed.reshape(16, 1, 8, LANES)]
        + [pltpu.roll(packed, LANES - 32 * q, 1).reshape(16, 1, 8, LANES) for q in range(1, 4)],
        axis=1,
    ).reshape(POINTS, LANES)
    lane = lanes_of(x.shape)
    x = jnp.where(lane < 32, x, 0.0)
    x_norm = -0.5 * jnp.sum(x * x, axis=1, keepdims=True)
    x = jnp.where((lane >= 32) & (lane < 35), 1.0, x)
    for k, part in enumerate(triple(x_norm)):
        x = jnp.where(lane == 35 + k, part, x)
    x = x[:, :DEPTH].astype(BF16)
    x_out[...] = x
    y = jnp.concatenate([samples_ref[k].astype(F32) for k in range(4)], axis=1)
    pot = jnp.sum(y[32:40], axis=0, keepdims=True)
    y = y[:32]
    y_norm = -0.5 * jnp.sum(y * y, axis=0, keepdims=True)
    shift = jnp.max(pot) - MARGIN
    y_out[:32, :] = y.astype(BF16)
    y_out[32:, :] = extra_rows(y_norm)
    y = jnp.concatenate([y.astype(BF16), extra_rows(y_norm + pot - shift)], axis=0)
    lines = []
    for tile in range(4):
        total = jnp.zeros((LANES, LANES), F32)
        left = x[tile * 128 : tile * 128 + 128]
        for chunk in range(8):
            right = y[:, chunk * 256 : chunk * 256 + 256]
            part = jnp.exp2(jnp.dot(left, right, preferred_element_type=F32) * SCALE)
            total += part[:, :LANES] + part[:, LANES:]
        line = jnp.transpose(total)
        line = jnp.sum(line, axis=0, keepdims=True)
        lines.append(jnp.log2(line) + SCALE * shift)
    lse_out[...] = jnp.broadcast_to(stack_up(lines)[None], (16, 4, LANES))


def col_pass(x_ref, y_ref, rows_ref, x_out, shift_out, sums_out, own_out):
    point = (LOG_SAMPLES - combine(rows_ref[...])) / SCALE
    z = lax.axis_index("z")
    z = sum(jnp.where(z == other, slot, 0) for slot, other in enumerate(Z_ORDER))
    line = jnp.sum(jnp.where(rows_of(point.shape) == z // 4, point, 0.0), axis=0, keepdims=True)
    line = pltpu.roll(jnp.broadcast_to(line, (8, LANES)), (4 - z % 4) * 32 % LANES, 1)
    own_out[...] = line[:1, :32]
    shift = jnp.max(point) - MARGIN
    shift_out[...] = jnp.full((1, LANES), shift, F32)
    parts = triple(point - shift)
    row = rows_of((DEPTH, LANES))
    blocks = []
    for tile in range(4):
        block = jnp.zeros((DEPTH, LANES), F32)
        for k, part in enumerate(parts):
            block = jnp.where(row == 38 + k, part[tile : tile + 1], block)
        blocks.append(jnp.transpose(block))
    x = (x_ref[...].astype(F32) + jnp.concatenate(blocks, axis=0)).astype(BF16)
    x_out[...] = x
    lines = []
    for chunk in range(8):
        right = y_ref[:, chunk * 256 : chunk * 256 + 256]
        total = jnp.zeros((8, 256), F32)
        for tile in range(4):
            left = x[tile * 128 : tile * 128 + 128]
            part = jnp.exp2(jnp.dot(left, right, preferred_element_type=F32) * SCALE)
            total += jnp.sum(part.reshape(16, 8, 256), axis=0)
        total = jnp.sum(total, axis=0, keepdims=True)
        lines += [total[:, :LANES], total[:, LANES:]]
    lane = lanes_of((8, LANES))
    block = jnp.zeros((8, LANES), F32)
    for k, part in enumerate(triple(jnp.full((1, LANES), shift, F32))):
        block = jnp.where(lane == k, part, block)
    block = jnp.concatenate([stack_up(lines), block], axis=0).astype(BF16)
    sums_out[...] = jnp.broadcast_to(block[None], (32, 24, LANES))


def weigh(x_ref, y_ref, shift_ref, cols_ref, parts_out, sample_out):
    cols = cols_ref[...].astype(F32)
    moved = jnp.sum(cols[:, 16:], axis=(1, 2), keepdims=True) / 8
    most = jnp.max(moved)
    total = jnp.sum(cols[:, :16] * jnp.exp2((moved - most) * SCALE), axis=0)
    sample = (LOG_POINTS - jnp.log2(total)) / SCALE - most
    side = lax.axis_index("x_hi") * 2 + lax.axis_index("core")
    own = sample[:4]
    for k in range(1, 4):
        own = jnp.where(side == k, sample[4 * k : 4 * k + 4], own)
    sample_out[...] = own
    y = y_ref[:32, :]
    y_norm = jnp.sum(y_ref[32:, :].astype(F32)[:3], axis=0, keepdims=True)
    shift = jnp.max(shift_ref[...])
    y_all = jnp.concatenate([y, extra_rows(y_norm + line_up(sample) + shift)], axis=0)
    x = x_ref[...]
    right = jnp.concatenate([y, y, y, y, jnp.ones((128, SAMPLES), BF16)], axis=0)
    shape = (8, 8, LANES)
    lane, row = lanes_of(shape), rows_of(shape)
    for tile in range(2):
        weights = []
        for chunk in range(8):
            cols = slice(chunk * 256, chunk * 256 + 256)
            part = jnp.dot(x[tile * 256 : tile * 256 + 256], y_all[:, cols], preferred_element_type=F32)
            weights.append(jnp.exp2(part * SCALE).astype(BF16))
        total = product(jnp.concatenate(weights, axis=1), right)
        numer = total[:, :LANES].reshape(8, 4, 8, LANES)
        denom = total[:, LANES:]
        denom = denom.reshape(8, 4, 8, 128)
        first, second = numer[:, 0], jnp.where(lane[:, :, :128] == row[:, :, :128], denom[:, 0], 0.0)
        for q in range(1, 4):
            first = jnp.where(lane // 32 == q, numer[:, q], first)
            second = jnp.where(lane[:, :, :128] == row[:, :, :128] + 8 * q, denom[:, q], second)
        second = jnp.sum(second, axis=1)
        for part in range(8):
            peer = Z_PARTS.index(Z_ORDER[tile * 8 + part])
            parts_out[9 * peer : 9 * peer + 8, :] = first[part]
            parts_out[9 * peer + 8 : 9 * peer + 9, :128] = second[part : part + 1]


def finish(parts_ref, bary_out):
    numer, denom = parts_ref[:8, :], parts_ref[8:9, :]
    for peer in range(1, 16):
        numer = numer + parts_ref[9 * peer : 9 * peer + 8, :]
        denom = denom + parts_ref[9 * peer + 8 : 9 * peer + 9, :]
    stack = [numer] + [pltpu.roll(numer, LANES - 32 * q, 1) for q in range(1, 4)]
    bary_out[...] = turned(jnp.concatenate(stack, axis=0))[:32, :32] / denom[:, :32]


Z_ORDER = (12, 13, 11, 14, 10, 15, 9, 0, 8, 1, 7, 2, 6, 3, 5, 4)
Z_ROWS = (9, 10, 8, 11, 7, 12, 6, 13, 5, 14, 4, 15, 3, 0, 2, 1)
Z_PARTS = (8, 9, 7, 10, 6, 11, 5, 12, 4, 13, 3, 14, 2, 15, 1, 0)
PLANE_ORDER = (10, 11, 6, 14, 24, 26, 7, 15, 25, 27, 2, 8, 20, 22, 28, 30, 3, 9, 21, 23, 29, 31, 4, 12, 16, 18, 5, 13, 17, 19, 0, 1)


def exchange(value, axes, order):
    return lax.all_to_all(value, axes, 0, 0, axis_index_groups=[list(order)])


def call(body, outs, *args):
    vmem = pl.BlockSpec(memory_space=pltpu.VMEM)
    return pl.pallas_call(
        body,
        out_shape=[jax.ShapeDtypeStruct(shape, dtype) for shape, dtype in outs],
        in_specs=[vmem] * len(args),
        out_specs=[vmem] * len(outs),
        compiler_params=pltpu.CompilerParams(vmem_limit_bytes=8 << 20),
    )(*args)


def on_device(points, samples, potential):
    (xs,) = call(prepare_points, [((16, 8, LANES), BF16)], points)
    xs = exchange(xs, "z", Z_ORDER).reshape(LANES, LANES)
    (own,) = call(prepare_samples, [((40, 512), BF16)], samples, potential.reshape(1, 512))
    near = [[0, 1, 6, 7], [4, 5, 2, 3]]
    ys = lax.all_gather(own, ("x_lo", "x_hi", "core"), axis_index_groups=near)
    x, y, rows = call(
        row_pass,
        [((POINTS, DEPTH), BF16), ((DEPTH, SAMPLES), BF16), ((16, 4, LANES), F32)],
        xs, ys,
    )
    rows = exchange(rows, "z", Z_ROWS)
    x, shift, cols, point = call(
        col_pass,
        [((POINTS, DEPTH), BF16), ((1, LANES), F32), ((32, 24, LANES), BF16), ((1, 32), F32)],
        x, y, rows,
    )
    cols = exchange(cols, PLANE, PLANE_ORDER)
    parts, sample = call(
        weigh, [((144, LANES), F32), ((4, LANES), F32)], x, y, shift, cols
    )
    parts = parts.reshape(16, 9, 1, LANES)
    parts = exchange(parts, "z", Z_PARTS).reshape(144, LANES)
    (bary,) = call(finish, [((32, 32), F32)], parts)
    return point.reshape(32), sample.reshape(512), bary


def solution(mesh):
    split = Mesh(mesh.devices.reshape(SHAPE), AXES)
    cols = ("z", "x_hi", "core")
    return jax.shard_map(
        on_device,
        mesh=split,
        in_specs=(P(None, AXES), P(None, cols), P(cols)),
        out_specs=(P(AXES), P(cols), P(None, AXES)),
        check_vma=False,
    )
```

```python
import math

import jax
import jax.numpy as jnp
from jax import lax
from jax.experimental import pallas as pl
from jax.experimental.pallas import tpu as pltpu
from jax.sharding import Mesh, PartitionSpec as P

EPS = 0.25
SCALE = math.log2(math.e) / EPS
MARGIN = 18.0
AXES = ("x_lo", "y", "z", "x_hi", "core")
SHAPE = (2, 4, 16, 2, 2)
PLANE = ("x_lo", "y", "x_hi", "core")
POINTS = 512
SAMPLES = 2048
LOG_POINTS = math.log2(POINTS * 32)
LOG_SAMPLES = math.log2(SAMPLES * 16)
LANES = 128
DEPTH = 48
F32 = jnp.float32
BF16 = jnp.bfloat16


def lanes_of(shape):
    return lax.broadcasted_iota(jnp.int32, shape, len(shape) - 1)


def rows_of(shape):
    return lax.broadcasted_iota(jnp.int32, shape, len(shape) - 2)


def triple(value):
    high = value.astype(BF16).astype(F32)
    rest = value - high
    mid = rest.astype(BF16).astype(F32)
    return high, mid, rest - mid


def turned(block):
    rows, cols = block.shape
    if rows < LANES:
        block = jnp.concatenate([block, jnp.zeros((LANES - rows, cols), block.dtype)], axis=0)
    return jnp.transpose(block)


def product(left, right):
    return lax.dot_general(left, right, (((1,), (1,)), ((), ())), preferred_element_type=F32)


def combine(lse):
    top = jnp.max(lse, axis=0)
    return top + jnp.log2(jnp.sum(jnp.exp2(lse - top[None]), axis=0))


def line_up(block):
    return jnp.concatenate([block[k : k + 1] for k in range(block.shape[0])], axis=1)


def stack_up(lines):
    lane = rows_of((len(lines), LANES))
    block = jnp.broadcast_to(lines[0], lane.shape)
    for k, line in enumerate(lines[1:], 1):
        block = jnp.where(lane == k, line, block)
    return block


def extra_rows(value):
    row = rows_of((16, value.shape[1]))
    block = jnp.where((row >= 3) & (row < 9), 1.0, 0.0)
    for k, part in enumerate(triple(value)):
        block = jnp.where(row == k, part, block)
    return block.astype(BF16)


def prepare_points(points_ref, points_out):
    x = turned(points_ref[...].astype(F32))
    packed = x[:8]
    for q in range(1, 4):
        packed = packed + pltpu.roll(x[8 * q : 8 * q + 8], 32 * q, 1)
    points_out[...] = jnp.broadcast_to(packed.astype(BF16)[None], (16, 8, LANES))


def prepare_samples(samples_ref, potential_ref, samples_out):
    samples_out[:32, :] = samples_ref[...]
    pot = potential_ref[...]
    row = rows_of((8, 512))
    block = jnp.zeros((8, 512), F32)
    for k, part in enumerate(triple(pot)):
        block = jnp.where(row == k, part, block)
    samples_out[32:, :] = block.astype(BF16)


def row_pass(points_ref, samples_ref, x_out, y_out, lse_out):
    packed = points_ref[...].astype(F32)
    x = jnp.concatenate(
        [packed.reshape(16, 1, 8, LANES)]
        + [pltpu.roll(packed, LANES - 32 * q, 1).reshape(16, 1, 8, LANES) for q in range(1, 4)],
        axis=1,
    ).reshape(POINTS, LANES)
    lane = lanes_of(x.shape)
    x = jnp.where(lane < 32, x, 0.0)
    x_norm = -0.5 * jnp.sum(x * x, axis=1, keepdims=True)
    x = jnp.where((lane >= 32) & (lane < 35), 1.0, x)
    for k, part in enumerate(triple(x_norm)):
        x = jnp.where(lane == 35 + k, part, x)
    x = x[:, :DEPTH].astype(BF16)
    x_out[...] = x
    y = jnp.concatenate([samples_ref[k].astype(F32) for k in (2, 3, 0, 1)], axis=1)
    pot = jnp.sum(y[32:40], axis=0, keepdims=True)
    y = y[:32]
    y_norm = -0.5 * jnp.sum(y * y, axis=0, keepdims=True)
    shift = jnp.max(pot) - MARGIN
    y_out[:32, :] = y.astype(BF16)
    y_out[32:, :] = extra_rows(y_norm)
    y = jnp.concatenate([y.astype(BF16), extra_rows(y_norm + pot - shift)], axis=0)
    lines = []
    for tile in range(4):
        total = jnp.zeros((LANES, LANES), F32)
        left = x[tile * 128 : tile * 128 + 128]
        for chunk in range(8):
            right = y[:, chunk * 256 : chunk * 256 + 256]
            part = jnp.exp2(jnp.dot(left, right, preferred_element_type=F32) * SCALE)
            total += part[:, :LANES] + part[:, LANES:]
        line = jnp.transpose(total)
        line = jnp.sum(line, axis=0, keepdims=True)
        lines.append(jnp.log2(line) + SCALE * shift)
    lse_out[...] = jnp.broadcast_to(stack_up(lines)[None], (16, 4, LANES))


def col_pass(x_ref, y_ref, rows_ref, x_out, shift_out, sums_out, own_out):
    point = (LOG_SAMPLES - combine(rows_ref[...])) / SCALE
    z = lax.axis_index("z")
    z = sum(jnp.where(z == other, slot, 0) for slot, other in enumerate(Z_ORDER))
    line = jnp.sum(jnp.where(rows_of(point.shape) == z // 4, point, 0.0), axis=0, keepdims=True)
    line = pltpu.roll(jnp.broadcast_to(line, (8, LANES)), (4 - z % 4) * 32 % LANES, 1)
    own_out[...] = line[:1, :32]
    shift = jnp.max(point) - MARGIN
    shift_out[...] = jnp.full((1, LANES), shift, F32)
    parts = triple(point - shift)
    row = rows_of((DEPTH, LANES))
    blocks = []
    for tile in range(4):
        block = jnp.zeros((DEPTH, LANES), F32)
        for k, part in enumerate(parts):
            block = jnp.where(row == 38 + k, part[tile : tile + 1], block)
        blocks.append(jnp.transpose(block))
    x = (x_ref[...].astype(F32) + jnp.concatenate(blocks, axis=0)).astype(BF16)
    x_out[...] = x
    lines = []
    for chunk in range(8):
        right = y_ref[:, chunk * 256 : chunk * 256 + 256]
        total = jnp.zeros((8, 256), F32)
        for tile in range(4):
            left = x[tile * 128 : tile * 128 + 128]
            part = jnp.exp2(jnp.dot(left, right, preferred_element_type=F32) * SCALE)
            total += jnp.sum(part.reshape(16, 8, 256), axis=0)
        total = jnp.sum(total, axis=0, keepdims=True)
        lines += [total[:, :LANES], total[:, LANES:]]
    lane = lanes_of((8, LANES))
    block = jnp.zeros((8, LANES), F32)
    for k, part in enumerate(triple(jnp.full((1, LANES), shift, F32))):
        block = jnp.where(lane == k, part, block)
    block = jnp.concatenate([stack_up(lines), block], axis=0).astype(BF16)
    sums_out[...] = jnp.broadcast_to(block[None], (32, 24, LANES))


def weigh(x_ref, y_ref, shift_ref, cols_ref, parts_out, sample_out):
    cols = cols_ref[...].astype(F32)
    moved = jnp.sum(cols[:, 16:], axis=(1, 2), keepdims=True) / 8
    most = jnp.max(moved)
    total = jnp.sum(cols[:, :16] * jnp.exp2((moved - most) * SCALE), axis=0)
    sample = (LOG_POINTS - jnp.log2(total)) / SCALE - most
    side = lax.axis_index("x_hi") * 2 + lax.axis_index("core")
    own = sample[:4]
    for k in range(1, 4):
        own = jnp.where(side == k, sample[4 * k : 4 * k + 4], own)
    sample_out[...] = own
    y = y_ref[:32, :]
    y_norm = jnp.sum(y_ref[32:, :].astype(F32)[:3], axis=0, keepdims=True)
    shift = jnp.max(shift_ref[...])
    y_all = jnp.concatenate([y, extra_rows(y_norm + line_up(sample) + shift)], axis=0)
    x = x_ref[...]
    right = jnp.concatenate([y, y, y, y, jnp.ones((128, SAMPLES), BF16)], axis=0)
    shape = (8, 8, LANES)
    lane, row = lanes_of(shape), rows_of(shape)
    for tile in range(2):
        weights = []
        for chunk in range(8):
            cols = slice(chunk * 256, chunk * 256 + 256)
            part = jnp.dot(x[tile * 256 : tile * 256 + 256], y_all[:, cols], preferred_element_type=F32)
            weights.append(jnp.exp2(part * SCALE).astype(BF16))
        total = product(jnp.concatenate(weights, axis=1), right)
        numer = total[:, :LANES].reshape(8, 4, 8, LANES)
        denom = total[:, LANES:]
        denom = denom.reshape(8, 4, 8, 128)
        first, second = numer[:, 0], jnp.where(lane[:, :, :128] == row[:, :, :128], denom[:, 0], 0.0)
        for q in range(1, 4):
            first = jnp.where(lane // 32 == q, numer[:, q], first)
            second = jnp.where(lane[:, :, :128] == row[:, :, :128] + 8 * q, denom[:, q], second)
        second = jnp.sum(second, axis=1)
        for part in range(8):
            peer = Z_PARTS.index(Z_ORDER[tile * 8 + part])
            parts_out[9 * peer : 9 * peer + 8, :] = first[part]
            parts_out[9 * peer + 8 : 9 * peer + 9, :128] = second[part : part + 1]


def finish(parts_ref, bary_out):
    numer, denom = parts_ref[:8, :], parts_ref[8:9, :]
    for peer in range(1, 16):
        numer = numer + parts_ref[9 * peer : 9 * peer + 8, :]
        denom = denom + parts_ref[9 * peer + 8 : 9 * peer + 9, :]
    stack = [numer] + [pltpu.roll(numer, LANES - 32 * q, 1) for q in range(1, 4)]
    bary_out[...] = turned(jnp.concatenate(stack, axis=0))[:32, :32] / denom[:, :32]


Z_ORDER = (12, 13, 11, 14, 10, 15, 9, 0, 8, 1, 7, 2, 6, 3, 5, 4)
Z_ROWS = (9, 10, 8, 11, 7, 12, 6, 13, 5, 14, 4, 15, 3, 0, 2, 1)
Z_PARTS = (8, 9, 7, 10, 6, 11, 5, 12, 4, 13, 3, 14, 2, 15, 1, 0)
PLANE_ORDER = (10, 11, 6, 14, 24, 26, 7, 15, 25, 27, 2, 8, 20, 22, 28, 30, 3, 9, 21, 23, 29, 31, 4, 12, 16, 18, 5, 13, 17, 19, 0, 1)


def exchange(value, axes, order):
    return lax.all_to_all(value, axes, 0, 0, axis_index_groups=[list(order)])


def call(body, outs, *args):
    vmem = pl.BlockSpec(memory_space=pltpu.VMEM)
    return pl.pallas_call(
        body,
        out_shape=[jax.ShapeDtypeStruct(shape, dtype) for shape, dtype in outs],
        in_specs=[vmem] * len(args),
        out_specs=[vmem] * len(outs),
        compiler_params=pltpu.CompilerParams(vmem_limit_bytes=8 << 20),
    )(*args)


def on_device(points, samples, potential):
    (xs,) = call(prepare_points, [((16, 8, LANES), BF16)], points)
    xs = exchange(xs, "z", Z_ORDER).reshape(LANES, LANES)
    (own,) = call(prepare_samples, [((40, 512), BF16)], samples, potential.reshape(1, 512))
    near = [[6, 7, 0, 1], [2, 3, 4, 5]]
    ys = lax.all_gather(own, ("x_lo", "x_hi", "core"), axis_index_groups=near)
    x, y, rows = call(
        row_pass,
        [((POINTS, DEPTH), BF16), ((DEPTH, SAMPLES), BF16), ((16, 4, LANES), F32)],
        xs, ys,
    )
    rows = exchange(rows, "z", Z_ROWS)
    x, shift, cols, point = call(
        col_pass,
        [((POINTS, DEPTH), BF16), ((1, LANES), F32), ((32, 24, LANES), BF16), ((1, 32), F32)],
        x, y, rows,
    )
    cols = exchange(cols, PLANE, PLANE_ORDER)
    parts, sample = call(
        weigh, [((144, LANES), F32), ((4, LANES), F32)], x, y, shift, cols
    )
    parts = parts.reshape(16, 9, 1, LANES)
    parts = exchange(parts, "z", Z_PARTS).reshape(144, LANES)
    (bary,) = call(finish, [((32, 32), F32)], parts)
    return point.reshape(32), sample.reshape(512), bary


def solution(mesh):
    split = Mesh(mesh.devices.reshape(SHAPE), AXES)
    cols = ("z", "x_hi", "core")
    return jax.shard_map(
        on_device,
        mesh=split,
        in_specs=(P(None, AXES), P(None, cols), P(cols)),
        out_specs=(P(AXES), P(cols), P(None, AXES)),
        check_vma=False,
    )
```

```python
import math

import jax
import jax.numpy as jnp
from jax import lax
from jax.experimental import pallas as pl
from jax.experimental.pallas import tpu as pltpu
from jax.sharding import Mesh, PartitionSpec as P

EPS = 0.25
SCALE = math.log2(math.e) / EPS
MARGIN = 18.0
AXES = ("x_lo", "y", "z", "x_hi", "core")
SHAPE = (2, 4, 16, 2, 2)
PLANE = ("x_lo", "y", "x_hi", "core")
POINTS = 512
SAMPLES = 2048
LOG_POINTS = math.log2(POINTS * 32)
LOG_SAMPLES = math.log2(SAMPLES * 16)
LANES = 128
DEPTH = 48
F32 = jnp.float32
BF16 = jnp.bfloat16


def lanes_of(shape):
    return lax.broadcasted_iota(jnp.int32, shape, len(shape) - 1)


def rows_of(shape):
    return lax.broadcasted_iota(jnp.int32, shape, len(shape) - 2)


def triple(value):
    high = value.astype(BF16).astype(F32)
    rest = value - high
    mid = rest.astype(BF16).astype(F32)
    return high, mid, rest - mid


def turned(block):
    rows, cols = block.shape
    if rows < LANES:
        block = jnp.concatenate([block, jnp.zeros((LANES - rows, cols), block.dtype)], axis=0)
    return jnp.transpose(block)


def product(left, right):
    return lax.dot_general(left, right, (((1,), (1,)), ((), ())), preferred_element_type=F32)


def combine(lse):
    top = jnp.max(lse, axis=0)
    return top + jnp.log2(jnp.sum(jnp.exp2(lse - top[None]), axis=0))


def line_up(block):
    return jnp.concatenate([block[k : k + 1] for k in range(block.shape[0])], axis=1)


def stack_up(lines):
    lane = rows_of((len(lines), LANES))
    block = jnp.broadcast_to(lines[0], lane.shape)
    for k, line in enumerate(lines[1:], 1):
        block = jnp.where(lane == k, line, block)
    return block


def extra_rows(value):
    row = rows_of((16, value.shape[1]))
    block = jnp.where((row >= 3) & (row < 9), 1.0, 0.0)
    for k, part in enumerate(triple(value)):
        block = jnp.where(row == k, part, block)
    return block.astype(BF16)


def prepare_points(points_ref, points_out):
    x = turned(points_ref[...].astype(F32))
    packed = x[:8]
    for q in range(1, 4):
        packed = packed + pltpu.roll(x[8 * q : 8 * q + 8], 32 * q, 1)
    points_out[...] = jnp.broadcast_to(packed.astype(BF16)[None], (16, 8, LANES))


def prepare_samples(samples_ref, potential_ref, samples_out):
    samples_out[:32, :] = samples_ref[...]
    pot = potential_ref[...]
    row = rows_of((8, 512))
    block = jnp.zeros((8, 512), F32)
    for k, part in enumerate(triple(pot)):
        block = jnp.where(row == k, part, block)
    samples_out[32:, :] = block.astype(BF16)


def row_pass(points_ref, samples_ref, x_out, y_out, lse_out):
    packed = points_ref[...].astype(F32)
    x = jnp.concatenate(
        [packed.reshape(16, 1, 8, LANES)]
        + [pltpu.roll(packed, LANES - 32 * q, 1).reshape(16, 1, 8, LANES) for q in range(1, 4)],
        axis=1,
    ).reshape(POINTS, LANES)
    lane = lanes_of(x.shape)
    x = jnp.where(lane < 32, x, 0.0)
    x_norm = -0.5 * jnp.sum(x * x, axis=1, keepdims=True)
    x = jnp.where((lane >= 32) & (lane < 35), 1.0, x)
    for k, part in enumerate(triple(x_norm)):
        x = jnp.where(lane == 35 + k, part, x)
    x = x[:, :DEPTH].astype(BF16)
    x_out[...] = x
    y = jnp.concatenate([samples_ref[k].astype(F32) for k in range(4)], axis=1)
    pot = jnp.sum(y[32:40], axis=0, keepdims=True)
    y = y[:32]
    y_norm = -0.5 * jnp.sum(y * y, axis=0, keepdims=True)
    shift = jnp.max(pot) - MARGIN
    y_out[:32, :] = y.astype(BF16)
    y_out[32:, :] = extra_rows(y_norm)
    y = jnp.concatenate([y.astype(BF16), extra_rows(y_norm + pot - shift)], axis=0)
    lines = []
    for tile in range(4):
        total = jnp.zeros((LANES, LANES), F32)
        left = x[tile * 128 : tile * 128 + 128]
        for chunk in range(8):
            right = y[:, chunk * 256 : chunk * 256 + 256]
            part = jnp.exp2(jnp.dot(left, right, preferred_element_type=F32) * SCALE)
            total += part[:, :LANES] + part[:, LANES:]
        line = jnp.transpose(total)
        line = jnp.sum(line, axis=0, keepdims=True)
        lines.append(jnp.log2(line) + SCALE * shift)
    lse_out[...] = jnp.broadcast_to(stack_up(lines)[None], (16, 4, LANES))


def col_pass(x_ref, y_ref, rows_ref, x_out, shift_out, sums_out, own_out):
    point = (LOG_SAMPLES - combine(rows_ref[...])) / SCALE
    z = lax.axis_index("z")
    z = sum(jnp.where(z == other, slot, 0) for slot, other in enumerate(Z_ORDER))
    line = jnp.sum(jnp.where(rows_of(point.shape) == z // 4, point, 0.0), axis=0, keepdims=True)
    line = pltpu.roll(jnp.broadcast_to(line, (8, LANES)), (4 - z % 4) * 32 % LANES, 1)
    own_out[...] = line[:1, :32]
    shift = jnp.max(point) - MARGIN
    shift_out[...] = jnp.full((1, LANES), shift, F32)
    parts = triple(point - shift)
    row = rows_of((DEPTH, LANES))
    blocks = []
    for tile in range(4):
        block = jnp.zeros((DEPTH, LANES), F32)
        for k, part in enumerate(parts):
            block = jnp.where(row == 38 + k, part[tile : tile + 1], block)
        blocks.append(jnp.transpose(block))
    x = (x_ref[...].astype(F32) + jnp.concatenate(blocks, axis=0)).astype(BF16)
    x_out[...] = x
    lines = []
    for chunk in range(8):
        right = y_ref[:, chunk * 256 : chunk * 256 + 256]
        total = jnp.zeros((8, 256), F32)
        for tile in range(4):
            left = x[tile * 128 : tile * 128 + 128]
            part = jnp.exp2(jnp.dot(left, right, preferred_element_type=F32) * SCALE)
            total += jnp.sum(part.reshape(16, 8, 256), axis=0)
        total = jnp.sum(total, axis=0, keepdims=True)
        lines += [total[:, :LANES], total[:, LANES:]]
    lane = lanes_of((8, LANES))
    block = jnp.zeros((8, LANES), F32)
    for k, part in enumerate(triple(jnp.full((1, LANES), shift, F32))):
        block = jnp.where(lane == k, part, block)
    block = jnp.concatenate([stack_up(lines), block], axis=0).astype(BF16)
    sums_out[...] = jnp.broadcast_to(block[None], (32, 24, LANES))


def weigh(x_ref, y_ref, shift_ref, cols_ref, parts_out, sample_out):
    cols = cols_ref[...].astype(F32)
    moved = jnp.sum(cols[:, 16:], axis=(1, 2), keepdims=True) / 8
    most = jnp.max(moved)
    total = jnp.sum(cols[:, :16] * jnp.exp2((moved - most) * SCALE), axis=0)
    sample = (LOG_POINTS - jnp.log2(total)) / SCALE - most
    side = lax.axis_index("x_hi") * 2 + lax.axis_index("core")
    own = sample[:4]
    for k in range(1, 4):
        own = jnp.where(side == k, sample[4 * k : 4 * k + 4], own)
    sample_out[...] = own
    y = y_ref[:32, :]
    y_norm = jnp.sum(y_ref[32:, :].astype(F32)[:3], axis=0, keepdims=True)
    shift = jnp.max(shift_ref[...])
    y_all = jnp.concatenate([y, extra_rows(y_norm + line_up(sample) + shift)], axis=0)
    x = x_ref[...]
    right = jnp.concatenate([y, y, y, y, jnp.ones((128, SAMPLES), BF16)], axis=0)
    shape = (8, 8, LANES)
    lane, row = lanes_of(shape), rows_of(shape)
    for tile in range(2):
        weights = []
        for chunk in range(8):
            cols = slice(chunk * 256, chunk * 256 + 256)
            part = jnp.dot(x[tile * 256 : tile * 256 + 256], y_all[:, cols], preferred_element_type=F32)
            weights.append(jnp.exp2(part * SCALE).astype(BF16))
        total = product(jnp.concatenate(weights, axis=1), right)
        numer = total[:, :LANES].reshape(8, 4, 8, LANES)
        denom = total[:, LANES:]
        denom = denom.reshape(8, 4, 8, 128)
        first, second = numer[:, 0], jnp.where(lane[:, :, :128] == row[:, :, :128], denom[:, 0], 0.0)
        for q in range(1, 4):
            first = jnp.where(lane // 32 == q, numer[:, q], first)
            second = jnp.where(lane[:, :, :128] == row[:, :, :128] + 8 * q, denom[:, q], second)
        second = jnp.sum(second, axis=1)
        for part in range(8):
            peer = Z_PARTS.index(Z_ORDER[tile * 8 + part])
            parts_out[9 * peer : 9 * peer + 8, :] = first[part]
            parts_out[9 * peer + 8 : 9 * peer + 9, :128] = second[part : part + 1]


def finish(parts_ref, bary_out):
    numer, denom = parts_ref[:8, :], parts_ref[8:9, :]
    for peer in range(1, 16):
        numer = numer + parts_ref[9 * peer : 9 * peer + 8, :]
        denom = denom + parts_ref[9 * peer + 8 : 9 * peer + 9, :]
    stack = [numer] + [pltpu.roll(numer, LANES - 32 * q, 1) for q in range(1, 4)]
    bary_out[...] = turned(jnp.concatenate(stack, axis=0))[:32, :32] / denom[:, :32]


Z_ORDER = (12, 13, 11, 14, 10, 15, 9, 0, 8, 1, 7, 2, 6, 3, 5, 4)
Z_ROWS = (9, 10, 8, 11, 7, 12, 6, 13, 5, 14, 4, 15, 3, 0, 2, 1)
Z_PARTS = (8, 9, 7, 10, 6, 11, 5, 12, 4, 13, 3, 14, 2, 15, 1, 0)
PLANE_ORDER = (11, 10, 7, 15, 25, 27, 6, 14, 24, 26, 3, 9, 21, 23, 29, 31, 2, 8, 20, 22, 28, 30, 5, 13, 17, 19, 4, 12, 16, 18, 1, 0)


def exchange(value, axes, order):
    return lax.all_to_all(value, axes, 0, 0, axis_index_groups=[list(order)])


def call(body, outs, *args):
    vmem = pl.BlockSpec(memory_space=pltpu.VMEM)
    return pl.pallas_call(
        body,
        out_shape=[jax.ShapeDtypeStruct(shape, dtype) for shape, dtype in outs],
        in_specs=[vmem] * len(args),
        out_specs=[vmem] * len(outs),
        compiler_params=pltpu.CompilerParams(vmem_limit_bytes=8 << 20),
    )(*args)


def on_device(points, samples, potential):
    (xs,) = call(prepare_points, [((16, 8, LANES), BF16)], points)
    xs = exchange(xs, "z", Z_ORDER).reshape(LANES, LANES)
    (own,) = call(prepare_samples, [((40, 512), BF16)], samples, potential.reshape(1, 512))
    near = [[0, 1, 6, 7], [4, 5, 2, 3]]
    ys = lax.all_gather(own, ("x_lo", "x_hi", "core"), axis_index_groups=near)
    x, y, rows = call(
        row_pass,
        [((POINTS, DEPTH), BF16), ((DEPTH, SAMPLES), BF16), ((16, 4, LANES), F32)],
        xs, ys,
    )
    rows = exchange(rows, "z", Z_ROWS)
    x, shift, cols, point = call(
        col_pass,
        [((POINTS, DEPTH), BF16), ((1, LANES), F32), ((32, 24, LANES), BF16), ((1, 32), F32)],
        x, y, rows,
    )
    cols = exchange(cols, PLANE, PLANE_ORDER)
    parts, sample = call(
        weigh, [((144, LANES), F32), ((4, LANES), F32)], x, y, shift, cols
    )
    parts = parts.reshape(16, 9, 1, LANES)
    parts = exchange(parts, "z", Z_PARTS).reshape(144, LANES)
    (bary,) = call(finish, [((32, 32), F32)], parts)
    return point.reshape(32), sample.reshape(512), bary


def solution(mesh):
    split = Mesh(mesh.devices.reshape(SHAPE), AXES)
    cols = ("z", "x_hi", "core")
    return jax.shard_map(
        on_device,
        mesh=split,
        in_specs=(P(None, AXES), P(None, cols), P(cols)),
        out_specs=(P(AXES), P(cols), P(None, AXES)),
        check_vma=False,
    )
```
